512 devices in a mesh: pop: 16 (over z), tp: 32 (over y, x, core).
Axes of the slice: x: 4, y: 4, z: 16, core: 2. Of those that a mesh axis runs over, the one named last changes fastest.
Arguments:
- in_spikes: int32 [4, 15, 4096], replicated, may hold values 0 or 1
- w_in: bfloat16 [4096, 4096], P(None, 'tp'), may hold values from -0.1875 to 0.1875
- w_rec: bfloat16 [4096, 4096], P(None, 'tp'), may hold values from -0.1875 to 0.1875
- leak_rate: float32 [4096], P('tp'), may hold values from 0.5 to 0.95
- neuron_bias: float32 [4096], P('tp'), may hold values from -2.5 to 2.5
- readout: float32 [4096], P('tp'), may hold values from -0.1875 to 0.1875
- pert_table: bfloat16 [256, 4096], P(None, 'tp'), may hold values from -4 to 4
- pert_idx: int32 [512, 2], P('pop'), may hold values from 0 to 255
- member_ranks: int32 [512], P('pop'), may hold values from 0 to 511, each once
Outputs:
- returns: float32 [512], P('pop')
- grad_rec: bfloat16 [4096, 4096], P(None, 'tp')
The draws below stay inside these ranges and needn't reach their ends.
Inputs may be any that keep to these rules, and one draw needn't show every extreme that they name: member_ranks holds each of 0 to 511 once.
All inputs are finite; a program needn't handle non-finite values.
Results may differ from the reference program's by a relative error of at most 0.0044.
Values may be sent and summed in bfloat16 or wider, within the bound.
A program may use at most 64 MiB of HBM per device.

```python
import jax
import jax.numpy as jnp
from jax import lax

NEUR = 4096
INP = 4096
KTAB = 256
STEPS = 4
EPIS = 15
MEMBERS = 512


def plant(array, stream_key, least, high):
    longest = array.shape.index(max(array.shape))
    spots = []
    for shift in (0, 1):
        where = [jax.random.randint(jax.random.fold_in(stream_key, axis), (), 0, length) for axis, length in enumerate(array.shape)]
        where[longest] = (where[longest] + shift) % array.shape[longest]
        spots.append(tuple(where))
    return array.at[spots[0]].set(least).at[spots[1]].set(high)


def shard_levels(key, dims, shards, smallest, largest):
    factor_of = 1.0
    for axis_at, blocks in shards:
        draws = jax.random.uniform(jax.random.fold_in(jax.random.fold_in(key, 6), axis_at), (blocks,), jnp.float32, smallest / len(shards), largest / len(shards))
        factor_of = factor_of * jnp.repeat(jnp.exp(draws), dims[axis_at] // blocks).reshape((-1,) + (1,) * (len(dims) - 1 - axis_at))
    return factor_of


def scatter_about(key, extent, spread, limit, cuts=(), dtype=jnp.bfloat16):
    array = jax.random.normal(key, extent, jnp.float32) * spread
    if len(cuts) > 0:
        array = shard_levels(key, extent, cuts, -0.22, 0.18) * array
    return jnp.clip(array, min=-limit, max=limit).astype(dtype)


def setup_inputs(seed: int = 0) -> dict:
    arg_keys = jax.random.split(jax.random.key(seed), 10)
    in_spikes = plant((jax.random.randint(arg_keys[0], (STEPS, EPIS, INP), 0, 4) < 1).astype(jnp.int32), jax.random.fold_in(arg_keys[0], 1), 0, 1)
    w_in = scatter_about(arg_keys[1], (INP, NEUR), (INP // 4) ** -0.5, 0.1875, ((1, 32),))
    w_rec = scatter_about(arg_keys[2], (NEUR, NEUR), (NEUR // 4) ** -0.5, 0.1875, ((1, 32),))
    leak_rate = jnp.clip(0.5 + 0.45 * jax.random.uniform(arg_keys[3], (NEUR,), jnp.float32) ** shard_levels(arg_keys[3], (NEUR,), ((0, 32),), -0.2, 0.2), 0.5, 0.95)
    neuron_bias = scatter_about(arg_keys[4], (NEUR,), 0.5, 2.5, ((0, 32),), jnp.float32)
    readout = scatter_about(arg_keys[5], (NEUR,), (NEUR // 4) ** -0.5, 0.1875, ((0, 32),), jnp.float32)
    pert_table = scatter_about(arg_keys[6], (KTAB, NEUR), 1.0, 4.0, ((1, 32),))
    pert_idx = plant(jax.random.randint(arg_keys[7], (MEMBERS, 2), 0, KTAB), jax.random.fold_in(arg_keys[7], 1), 0, KTAB - 1).astype(jnp.int32)
    member_ranks = jax.random.permutation(arg_keys[8], MEMBERS).astype(jnp.int32)
    return {"in_spikes": in_spikes, "w_in": w_in, "w_rec": w_rec, "leak_rate": leak_rate, "neuron_bias": neuron_bias, "readout": readout, "pert_table": pert_table, "pert_idx": pert_idx, "member_ranks": member_ranks}


sigma_scale = 0.01

def reference(in_spikes, w_in, w_rec, leak_rate, neuron_bias, readout, pert_table, pert_idx, member_ranks):
    member_count = pert_idx.shape[0]
    spike_input = in_spikes.astype(jnp.bfloat16).reshape(STEPS * EPIS, INP)
    input_drive = jnp.dot(spike_input, w_in, preferred_element_type=jnp.float32) + neuron_bias
    input_drive = input_drive.reshape(STEPS, EPIS, NEUR)
    pre_side = jnp.take(pert_table, pert_idx[:, 0], axis=0)
    post_side = jnp.take(pert_table, pert_idx[:, 1], axis=0).astype(jnp.float32)
    membrane = jnp.zeros((member_count, EPIS, NEUR), jnp.float32)
    spikes = jnp.zeros((member_count, EPIS, NEUR), jnp.bfloat16)
    readout_sum = jnp.zeros((member_count, EPIS), jnp.float32)
    for moment in range(STEPS):
        current = jnp.broadcast_to(input_drive[moment][None], membrane.shape)
        if moment > 0:
            recurrent = jnp.dot(spikes.reshape(member_count * EPIS, NEUR), w_rec, preferred_element_type=jnp.float32)
            projection = jnp.einsum('men,mn->me', spikes.astype(jnp.float32), pre_side.astype(jnp.float32), precision=lax.Precision.HIGHEST)
            current = current + recurrent.reshape(member_count, EPIS, NEUR) + sigma_scale * projection[:, :, None] * post_side[:, None, :]
        membrane = leak_rate * (membrane - spikes.astype(jnp.float32)) + current
        spikes = jax.nn.sigmoid(4.0 * (membrane - 1.0)).astype(jnp.bfloat16)
        readout_sum = readout_sum + jnp.einsum('men,n->me', spikes.astype(jnp.float32), readout, precision=lax.Precision.HIGHEST)
    returns = lax.optimization_barrier(jnp.sum(readout_sum, axis=1)) / (EPIS * STEPS)
    fitness = member_ranks.astype(jnp.float32) / (member_count - 1) - 0.5 + returns
    weighted = pre_side.astype(jnp.float32) * fitness[:, None]
    grad_rec = jnp.dot(weighted.T, post_side, precision=lax.Precision.HIGHEST) * jnp.sqrt(12.0 / member_count)
    return (returns, grad_rec.astype(jnp.bfloat16))
```

```python
import functools

import jax
import jax.numpy as jnp
from jax import lax
from jax.experimental import pallas as pl
from jax.experimental.pallas import tpu as pltpu
from jax.sharding import PartitionSpec as P

MESH = pl.DeviceIdType.MESH
F32 = jnp.float32
BF16 = jnp.bfloat16
sigma_scale = 0.01

STEPS = 4
EPIS = 15
EP = 16
SIDE = 4
CHIPS = 16
TP = 32
COLS = 128
PAIR = 256
HALF = 16
ROWS = EPIS * HALF
NEUR = 4096
KTAB = 256

NT = (((1,), (1,)), ((), ()))
TN = (((0,), (0,)), ((), ()))


def dot(left, right):
    return jnp.dot(left, right, preferred_element_type=F32)


def dot_nt(left, right):
    return lax.dot_general(left, right, NT, preferred_element_type=F32)


def squash(membrane):
    return (0.5 + 0.5 * jnp.tanh(2.0 * membrane - 2.0)).astype(BF16)


def kernel(
    pops,
    in_hbm,
    w_in_hbm,
    w_rec_hbm,
    leak_ref,
    bias_ref,
    readout_ref,
    table_hbm,
    idx_ref,
    rank_ref,
    returns_ref,
    grad_hbm,
    spk_v,
    w_in_v,
    w_pair,
    x_v,
    table_v,
    tt_all,
    m1_src,
    m1,
    m2,
    pair_v,
    meta,
    m3,
    m4,
    proj_v,
    lhs_v,
    acc_v,
    accp_v,
    mem_v,
    spikes_v,
    post_all,
    grad_v,
    local_sem,
    out_sem,
    m1_send,
    m1_recv,
    m2_send,
    m2_recv,
    m3_send,
    m3_recv,
    m4_send,
    m4_recv,
    meta_send,
    meta_recv,
    pair_send,
    pair_recv,
    tt_send,
    tt_recv,
    sp_send,
    sp_recv,
):
    pop = lax.axis_index("pop")
    me = lax.axis_index("tp")
    core = lax.rem(me, 2)
    chip = lax.div(me, 2)
    mate = me + 1 - 2 * core
    groups = max(1, pops // 4)

    loads = [
        pltpu.make_async_copy(src, dst, local_sem.at[i])
        for i, (src, dst) in enumerate(
            (
                (in_hbm, spk_v),
                (w_in_hbm, w_in_v),
                (table_hbm, table_v),
                (w_rec_hbm, w_pair.at[core]),
            )
        )
    ]
    for load in loads:
        load.start()

    barrier = pltpu.get_barrier_semaphore()

    def greet_plane(k, _):
        pl.semaphore_signal(
            barrier, inc=1, device_id=(pop, lax.rem(me + k, TP)), device_id_type=MESH
        )
        return 0

    lax.fori_loop(1, TP, greet_plane, 0)

    def greet_pop(k, _):
        pl.semaphore_signal(
            barrier, inc=1, device_id=(lax.rem(pop + k, pops), me), device_id_type=MESH
        )
        return 0

    if pops > 1:
        lax.fori_loop(1, pops, greet_pop, 0)

    lane = lax.broadcasted_iota(jnp.int32, (32, 128), 1)
    member = lax.broadcasted_iota(jnp.int32, (32, 128), 0)
    here = lane == member + lax.rem(pop, 4) * 32
    pre_idx = idx_ref[:, 0:1]
    post_idx = idx_ref[:, 1:2]
    pre_row = jnp.sum(jnp.where(here, pre_idx.astype(F32), 0.0), axis=0, keepdims=True)
    post_row = jnp.sum(jnp.where(here, post_idx.astype(F32), 0.0), axis=0, keepdims=True)
    meta[pop, 0:1, :] = pre_row
    meta[pop, 1:2, :] = post_row
    meta[pop, 2:8, :] = jnp.zeros((6, 128), F32)

    loads[2].wait()
    spot = lax.broadcasted_iota(jnp.int32, (32, KTAB), 1)
    pick = jnp.concatenate(
        [
            jnp.where(spot == pre_idx, 1.0, 0.0).astype(BF16),
            jnp.where(spot == post_idx, 1.0, 0.0).astype(BF16),
        ],
        axis=0,
    )
    picked = dot(pick, table_v[...]).astype(BF16)
    for half in range(2):
        m1_src[half, 16:32, :] = picked[16 * half : 16 * half + 16]
        m1_src[half, 32:48, :] = picked[32 + 16 * half : 48 + 16 * half]
    tt_all[core, chip] = table_v[...].astype(F32).T.astype(BF16)

    loads[0].wait()
    for t in range(STEPS):
        rows = spk_v[t].astype(F32)
        x_v[EP * t : EP * (t + 1), :] = jnp.concatenate(
            [rows, jnp.zeros((EP - EPIS, NEUR), F32)], axis=0
        ).astype(BF16)
    loads[1].wait()
    drive = dot(x_v[...], w_in_v[...]) + bias_ref[...]
    drive0 = drive[0:16]
    drive1 = drive[16:32]
    pair_v[core, 0:32, :] = drive[32:64]
    pair_v[core, 32:40, :] = jnp.broadcast_to(leak_ref[...], (8, 128))
    pair_v[core, 40:48, :] = jnp.broadcast_to(readout_ref[...], (8, 128))
    spikes0 = squash(drive0)
    m1_src[0, 0:16, :] = spikes0
    m1_src[1, 0:16, :] = spikes0
    m1[me] = m1_src[core]

    pl.semaphore_wait(barrier, TP - 1 + pops - 1)

    def send_m1(k, _):
        peer = lax.rem(me + k, TP)
        pltpu.make_async_remote_copy(
            src_ref=m1_src.at[lax.rem(peer, 2)],
            dst_ref=m1.at[me],
            send_sem=m1_send,
            recv_sem=m1_recv,
            device_id=(pop, peer),
            device_id_type=MESH,
        ).start()
        return 0

    lax.fori_loop(1, TP, send_m1, 0)

    to_mate = [
        pltpu.make_async_remote_copy(
            src_ref=src,
            dst_ref=dst,
            send_sem=pair_send.at[i],
            recv_sem=pair_recv.at[i],
            device_id=(pop, mate),
            device_id_type=MESH,
        )
        for i, (src, dst) in enumerate(
            (
                (pair_v.at[core], pair_v.at[core]),
                (w_rec_hbm, w_pair.at[core]),
                (tt_all.at[core], tt_all.at[core]),
            )
        )
    ]
    to_mate[0].start()
    to_mate[1].start()

    first = lax.rem(chip, SIDE) * (1 - core) + lax.div(chip, SIDE) * core
    second = lax.div(chip, SIDE) * (1 - core) + lax.rem(chip, SIDE) * core

    def chip_at(u, v):
        return (u * (1 - core) + v * core) + SIDE * (v * (1 - core) + u * core)

    def step(w, by):
        return lax.rem(w + by, SIDE)

    across = [first, step(first, 3), step(first, 1), step(first, 2)]
    v_minus, v_plus, v_far = step(second, 3), step(second, 1), step(second, 2)

    def gather_ops(ref, low, send_sem, recv_sem):
        total = ref.shape[1]

        def part(slot, half):
            if half == 0:
                return ref.at[slot, pl.ds(0, low)]
            if half == 1:
                return ref.at[slot, pl.ds(low, total - low)]
            return ref.at[slot]

        def send(slot, to, sem, half=None):
            pltpu.make_async_remote_copy(
                src_ref=part(slot, half),
                dst_ref=part(slot, half),
                send_sem=send_sem,
                recv_sem=recv_sem.at[sem],
                device_id=(pop, 2 * to + core),
                device_id_type=MESH,
            ).start()

        def wait(slot, sem, half=None):
            piece = part(slot, half)
            pltpu.make_async_copy(piece, piece, recv_sem.at[sem]).wait()

        def along(i):
            slot = chip_at(across[i], second)
            send(slot, chip_at(first, v_plus), 4 + 4 * i)
            send(slot, chip_at(first, v_minus), 5 + 4 * i)

        def begin():
            slot = chip_at(first, second)
            send(slot, chip_at(across[2], second), 0)
            send(slot, chip_at(across[1], second), 1)
            along(0)

        def near(i):
            slot = chip_at(across[i], second)
            wait(slot, i - 1)
            send(slot, chip_at(across[3 - i], second), 1 + i, half=i - 1)
            along(i)
            return slot

        def far():
            slot = chip_at(across[3], second)
            wait(slot, 2, half=0)
            wait(slot, 3, half=1)
            along(3)
            return slot

        def side_minus(i):
            slot = chip_at(across[i], v_minus)
            wait(slot, 4 + 4 * i)
            send(slot, chip_at(first, v_plus), 6 + 4 * i, half=0)
            return slot

        def side_plus(i):
            slot = chip_at(across[i], v_plus)
            wait(slot, 5 + 4 * i)
            send(slot, chip_at(first, v_minus), 7 + 4 * i, half=1)
            return slot

        def last(i):
            slot = chip_at(across[i], v_far)
            wait(slot, 6 + 4 * i, half=0)
            wait(slot, 7 + 4 * i, half=1)
            return slot

        def finish():
            sent = ref.at[pl.ds(0, CHIPS - 1)]
            pltpu.make_async_copy(sent, sent, send_sem).wait()

        return begin, near, far, side_minus, side_plus, last, finish

    tt_ref = tt_all.at[core]
    tt_begin, tt_near, tt_far, tt_minus, tt_plus, tt_last, tt_finish = gather_ops(
        tt_ref, 64, tt_send, tt_recv
    )
    tt_begin()

    def send_meta(k, _):
        pltpu.make_async_remote_copy(
            src_ref=meta.at[pop],
            dst_ref=meta.at[pop],
            send_sem=meta_send,
            recv_sem=meta_recv,
            device_id=(lax.rem(pop + k, pops), me),
            device_id_type=MESH,
        ).start()
        return 0

    if pops > 1:
        lax.fori_loop(1, pops, send_meta, 0)

    loads[3].wait()
    others = m1.at[pl.ds(0, TP - 1)]
    pltpu.make_async_copy(others, others, m1_recv).wait()

    def both(ref, c, low, high):
        return jnp.concatenate([ref[2 * c, low:high, :], ref[2 * c + 1, low:high, :]], axis=1)

    recurrent1 = jnp.zeros((16, COLS), F32)
    for c in range(CHIPS):
        recurrent1 = recurrent1 + dot(
            both(m1, c, 0, 16), w_pair[core, pl.ds(PAIR * c, PAIR), :]
        )
    m2[me] = leak_ref[...] * (drive0 - spikes0.astype(F32)) + (drive1 + recurrent1)

    def send_m2(k, _):
        pltpu.make_async_remote_copy(
            src_ref=m2.at[me],
            dst_ref=m2.at[me],
            send_sem=m2_send,
            recv_sem=m2_recv,
            device_id=(pop, lax.rem(me + k, TP)),
            device_id_type=MESH,
        ).start()
        return 0

    lax.fori_loop(1, TP, send_m2, 0)

    project1 = jnp.zeros((HALF, EP), F32)
    for c in range(CHIPS):
        project1 = project1 + dot_nt(both(m1, c, 16, 32), both(m1, c, 0, 16))
    for e in range(EPIS):
        proj_v[e] = jnp.broadcast_to(sigma_scale * project1[:, e : e + 1], (HALF, 128))

    tt_near(1)
    tt_near(2)
    tt_minus(0)
    tt_plus(0)

    to_mate[0].wait_recv()
    to_mate[1].wait_recv()
    others2 = m2.at[pl.ds(0, TP - 1)]
    pltpu.make_async_copy(others2, others2, m2_recv).wait()

    acc_v[...] = jnp.zeros_like(acc_v)
    accp_v[...] = jnp.zeros_like(accp_v)

    def weights(c):
        rows = pl.ds(pl.multiple_of(PAIR * c, PAIR), PAIR)
        return jnp.concatenate([w_pair[0, rows, :], w_pair[1, rows, :]], axis=1)

    def spread(e):
        return jnp.concatenate([proj_v[e], proj_v[e]], axis=1)

    def step2(i, _):
        for k in range(2):
            c = 2 * i + k
            base = 2.0 * both(m2, c, 0, 16) - 2.0
            post = 2.0 * both(m1, c, 32, 48).astype(F32)
            for e in range(EPIS):
                lhs_v[k, HALF * e : HALF * (e + 1), :] = (
                    0.5 + 0.5 * jnp.tanh(base[e : e + 1] + spread(e) * post)
                ).astype(BF16)
        for k in range(2):
            c = 2 * i + k
            acc_v[...] += dot(lhs_v[k], weights(c))
            accp_v[...] += dot_nt(lhs_v[k], both(m1, c, 16, 32))
        return 0

    lax.fori_loop(0, CHIPS // 2, step2, 0)

    leak = jnp.concatenate([pair_v[0, 32:33, :], pair_v[1, 32:33, :]], axis=1)
    readout = jnp.concatenate([pair_v[0, 40:41, :], pair_v[1, 40:41, :]], axis=1)
    drive2 = jnp.concatenate([pair_v[0, 0:16, :], pair_v[1, 0:16, :]], axis=1)
    drive3 = jnp.concatenate([pair_v[0, 16:32, :], pair_v[1, 16:32, :]], axis=1)
    post_here = both(m1, chip, 32, 48).astype(F32)
    base_here = both(m2, chip, 0, 16)
    eye = lax.broadcasted_iota(jnp.int32, (HALF, HALF), 0) == lax.broadcasted_iota(
        jnp.int32, (HALF, HALF), 1
    )

    def projection(e):
        square = accp_v[HALF * e : HALF * (e + 1), :]
        own = jnp.sum(jnp.where(eye, square, 0.0), axis=1, keepdims=True)
        return sigma_scale * own * post_here

    first_spikes = both(m1, chip, 0, 16).astype(F32)
    real = lax.broadcasted_iota(jnp.int32, (EP, PAIR), 0) < EPIS
    spike_sum = jnp.broadcast_to(
        jnp.sum(jnp.where(real, first_spikes, 0.0), axis=0, keepdims=True), (HALF, PAIR)
    )
    for e in range(EPIS):
        rows = slice(HALF * e, HALF * (e + 1))
        membrane1 = base_here[e : e + 1] + spread(e) * post_here
        spikes1 = squash(membrane1).astype(F32)
        membrane2 = leak * (membrane1 - spikes1) + (
            drive2[e : e + 1] + acc_v[rows, :] + projection(e)
        )
        spikes2 = squash(membrane2)
        spikes_v[chip, rows, :] = spikes2
        wide = spikes2.astype(F32)
        spike_sum = spike_sum + (spikes1 + wide)
        mem_v[rows, :] = leak * (membrane2 - wide) + drive3[e : e + 1]

    sp_begin, sp_near, sp_far, sp_minus, sp_plus, sp_last, sp_finish = gather_ops(
        spikes_v, 128, sp_send, sp_recv
    )
    sp_begin()

    acc_v[...] = jnp.zeros_like(acc_v)
    accp_v[...] = jnp.zeros_like(accp_v)

    def take(c):
        block = spikes_v[c]
        acc_v[...] += dot(block, weights(c))
        accp_v[...] += dot_nt(block, both(m1, c, 16, 32))

    tt_far()
    take(chip)
    take(sp_near(1))
    take(sp_near(2))
    take(sp_minus(0))
    take(sp_plus(0))
    take(sp_far())
    tt_minus(1)
    tt_plus(1)
    tt_minus(2)
    tt_plus(2)
    take(sp_minus(1))
    take(sp_plus(1))
    take(sp_minus(2))
    take(sp_plus(2))
    take(sp_last(0))
    tt_minus(3)
    tt_plus(3)
    take(sp_minus(3))
    take(sp_plus(3))

    if pops > 1:
        others3 = meta.at[pl.ds(0, pops - 1)]
        pltpu.make_async_copy(others3, others3, meta_recv).wait()
    slot_of = lax.broadcasted_iota(jnp.int32, (KTAB, 128), 0).astype(F32)
    per_group = min(4, pops)

    def group_row(ref, g, row):
        total = ref[per_group * g, row : row + 1, :]
        for k in range(1, per_group):
            total = total + ref[per_group * g + k, row : row + 1, :]
        return total

    for g in range(groups):
        chosen = jnp.where(slot_of == group_row(meta, g, 1), 1.0, 0.0)
        post_all[128 * g : 128 * (g + 1), :] = dot(
            chosen.T.astype(BF16), table_v[...]
        ).astype(BF16)

    take(sp_last(1))
    take(sp_last(2))
    take(sp_last(3))

    for e in range(EPIS):
        rows = slice(HALF * e, HALF * (e + 1))
        membrane3 = mem_v[rows, :] + (acc_v[rows, :] + projection(e))
        spike_sum = spike_sum + squash(membrane3).astype(F32)

    reward = jnp.sum(spike_sum * readout, axis=1, keepdims=True)
    lane16 = lax.broadcasted_iota(jnp.int32, (HALF, 128), 1)
    member16 = lax.broadcasted_iota(jnp.int32, (HALF, 128), 0)
    mine = lane16 == member16 + (lax.rem(pop, 4) * 32 + core * HALF)
    m3[me] = jnp.sum(jnp.where(mine, reward, 0.0), axis=0, keepdims=True)

    def send_m3(k, _):
        pltpu.make_async_remote_copy(
            src_ref=m3.at[me],
            dst_ref=m3.at[me],
            send_sem=m3_send,
            recv_sem=m3_recv,
            device_id=(pop, lax.rem(me + k, TP)),
            device_id_type=MESH,
        ).start()
        return 0

    lax.fori_loop(1, TP, send_m3, 0)

    for i in range(4):
        tt_last(i)
    to_mate[2].start()

    others4 = m3.at[pl.ds(0, TP - 1)]
    pltpu.make_async_copy(others4, others4, m3_recv).wait()
    returns_row = jnp.sum(m3[...], axis=0) / (EPIS * STEPS)
    returns_ref[...] = (
        returns_row[:, 0:32] + returns_row[:, 32:64] + returns_row[:, 64:96] + returns_row[:, 96:128]
    )
    ranks = rank_ref[...].astype(F32) / (32 * pops - 1) - 0.5
    ranks = jnp.concatenate([ranks, ranks, ranks, ranks], axis=1)
    lane1 = lax.broadcasted_iota(jnp.int32, (1, 128), 1)
    m4[pop] = jnp.where(lax.div(lane1, 32) == lax.rem(pop, 4), ranks + returns_row, 0.0)

    def send_m4(k, _):
        pltpu.make_async_remote_copy(
            src_ref=m4.at[pop],
            dst_ref=m4.at[pop],
            send_sem=m4_send,
            recv_sem=m4_recv,
            device_id=(lax.rem(pop + k, pops), me),
            device_id_type=MESH,
        ).start()
        return 0

    if pops > 1:
        lax.fori_loop(1, pops, send_m4, 0)
        others5 = m4.at[pl.ds(0, pops - 1)]
        pltpu.make_async_copy(others5, others5, m4_recv).wait()

    high, low = [], []
    for g in range(groups):
        scaled = jnp.where(slot_of == group_row(meta, g, 0), group_row(m4, g, 0), 0.0)
        top = scaled.astype(BF16)
        high.append(top)
        low.append((scaled - top.astype(F32)).astype(BF16))
    mixed = dot(jnp.concatenate(high, axis=1), post_all[...]) + dot(
        jnp.concatenate(low, axis=1), post_all[...]
    )
    mixed = mixed * jnp.sqrt(jnp.float32(12.0 / (32 * pops)))
    top = mixed.astype(BF16)
    split = jnp.concatenate([top, (mixed - top.astype(F32)).astype(BF16)], axis=1)

    to_mate[2].wait_recv()

    def grad_rows(c, _):
        for k in range(2):
            both_parts = dot(tt_all[k, c], split)
            start = pl.multiple_of(PAIR * c + COLS * k, COLS)
            grad_v[pl.ds(start, COLS), :] = (
                both_parts[:, 0:COLS] + both_parts[:, COLS:PAIR]
            ).astype(BF16)
        return 0

    stores = []
    for q in range(4):
        lax.fori_loop(4 * q, 4 * q + 4, grad_rows, 0)
        store = pltpu.make_async_copy(
            grad_v.at[pl.ds(1024 * q, 1024)], grad_hbm.at[pl.ds(1024 * q, 1024)], out_sem.at[q]
        )
        store.start()
        stores.append(store)

    tt_finish()
    sp_finish()
    pltpu.make_async_copy(others, others, m1_send).wait()
    pltpu.make_async_copy(others2, others2, m2_send).wait()
    pltpu.make_async_copy(others4, others4, m3_send).wait()
    if pops > 1:
        pltpu.make_async_copy(others3, others3, meta_send).wait()
        pltpu.make_async_copy(others5, others5, m4_send).wait()
    for copy in to_mate:
        copy.wait_send()
    for store in stores:
        store.wait()


def shards(
    in_spikes, w_in, w_rec, leak_rate, neuron_bias, readout, pert_table, pert_idx, member_ranks
):
    pops = lax.axis_size("pop")
    vmem = pl.BlockSpec(memory_space=pltpu.VMEM)
    hbm = pl.BlockSpec(memory_space=pl.ANY)
    dma = pltpu.SemaphoreType.DMA
    returns, grad_rec = pl.pallas_call(
        functools.partial(kernel, pops),
        out_shape=(
            jax.ShapeDtypeStruct((1, 32), F32),
            jax.ShapeDtypeStruct((NEUR, COLS), BF16),
        ),
        in_specs=[hbm, hbm, hbm, vmem, vmem, vmem, hbm, vmem, vmem],
        out_specs=(vmem, hbm),
        scratch_shapes=[
            pltpu.VMEM((STEPS, EPIS, NEUR), jnp.int32),
            pltpu.VMEM((NEUR, COLS), BF16),
            pltpu.VMEM((2, NEUR, COLS), BF16),
            pltpu.VMEM((STEPS * EP, NEUR), BF16),
            pltpu.VMEM((KTAB, COLS), BF16),
            pltpu.VMEM((2, CHIPS, COLS, KTAB), BF16),
            pltpu.VMEM((2, 48, COLS), BF16),
            pltpu.VMEM((TP, 48, COLS), BF16),
            pltpu.VMEM((TP, EP, COLS), F32),
            pltpu.VMEM((2, 48, COLS), F32),
            pltpu.VMEM((pops, 8, 128), F32),
            pltpu.VMEM((TP, 1, 128), F32),
            pltpu.VMEM((pops, 1, 128), F32),
            pltpu.VMEM((EPIS, HALF, 128), F32),
            pltpu.VMEM((2, ROWS, PAIR), BF16),
            pltpu.VMEM((ROWS, PAIR), F32),
            pltpu.VMEM((ROWS, HALF), F32),
            pltpu.VMEM((ROWS, PAIR), F32),
            pltpu.VMEM((CHIPS, ROWS, PAIR), BF16),
            pltpu.VMEM((128 * max(1, pops // 4), COLS), BF16),
            pltpu.VMEM((NEUR, COLS), BF16),
            dma((4,)),
            dma((4,)),
            dma,
            dma,
            dma,
            dma,
            dma,
            dma,
            dma,
            dma,
            dma,
            dma,
            dma((3,)),
            dma((3,)),
            dma,
            dma((20,)),
            dma,
            dma((20,)),
        ],
        compiler_params=pltpu.CompilerParams(
            collective_id=0, has_side_effects=True, vmem_limit_bytes=48 * 1024 * 1024
        ),
        name="rollout",
    )(
        in_spikes,
        w_in,
        w_rec,
        leak_rate.reshape(1, COLS),
        neuron_bias.reshape(1, COLS),
        readout.reshape(1, COLS),
        pert_table,
        pert_idx,
        member_ranks.reshape(1, 32),
    )
    return returns.reshape(32), grad_rec


def solution(mesh):
    placed = (
        P(),
        P(None, "tp"),
        P(None, "tp"),
        P("tp"),
        P("tp"),
        P("tp"),
        P(None, "tp"),
        P("pop", None),
        P("pop"),
    )
    return jax.shard_map(
        shards, mesh=mesh, in_specs=placed, out_specs=(P("pop"), P(None, "tp")), check_vma=False
    )
```

```python
import functools

import jax
import jax.numpy as jnp
from jax import lax
from jax.experimental import pallas as pl
from jax.experimental.pallas import tpu as pltpu
from jax.sharding import PartitionSpec as P

MESH = pl.DeviceIdType.MESH
F32 = jnp.float32
BF16 = jnp.bfloat16
sigma_scale = 0.01

STEPS = 4
EPIS = 15
EP = 16
SIDE = 4
CHIPS = 16
TP = 32
COLS = 128
PAIR = 256
HALF = 16
ROWS = EPIS * HALF
PIECES = 3
PIECE = ROWS // PIECES
NEUR = 4096
KTAB = 256

NT = (((1,), (1,)), ((), ()))
TN = (((0,), (0,)), ((), ()))


def dot(left, right):
    return jnp.dot(left, right, preferred_element_type=F32)


def dot_nt(left, right):
    return lax.dot_general(left, right, NT, preferred_element_type=F32)


def squash(membrane):
    return (0.5 + 0.5 * jnp.tanh(2.0 * membrane - 2.0)).astype(BF16)


def kernel(
    pops,
    in_hbm,
    w_in_hbm,
    w_rec_hbm,
    leak_ref,
    bias_ref,
    readout_ref,
    table_hbm,
    idx_ref,
    rank_ref,
    returns_ref,
    grad_ref,
    spk_v,
    w_in_v,
    w_pair,
    x_v,
    drive_v,
    table_v,
    tt_all,
    rows_src,
    rows_v,
    m1,
    m2,
    pair_v,
    meta,
    m3,
    m4,
    proj_v,
    lhs_v,
    acc_v,
    accp_v,
    mem_v,
    spikes_v,
    post_all,
    local_sem,
    m1_send,
    m1_recv,
    rows_send,
    rows_recv,
    m2_send,
    m2_recv,
    m3_send,
    m3_recv,
    m4_send,
    m4_recv,
    meta_send,
    meta_recv,
    pair_send,
    pair_recv,
    tt_send,
    tt_recv,
    sp_send,
    sp_recv,
):
    pop = lax.axis_index("pop")
    me = lax.axis_index("tp")
    core = lax.rem(me, 2)
    chip = lax.div(me, 2)
    mate = me + 1 - 2 * core
    groups = max(1, pops // 4)
    quarter = NEUR // 4
    parts = [pl.ds(quarter * q, quarter) for q in range(4)]
    loads = [pltpu.make_async_copy(table_hbm, table_v, local_sem.at[0])]
    for q, part in enumerate(parts):
        loads += [
            pltpu.make_async_copy(
                in_hbm.at[:, :, part], spk_v.at[:, :, part], local_sem.at[2 * q + 1]
            ),
            pltpu.make_async_copy(w_in_hbm.at[part], w_in_v.at[part], local_sem.at[2 * q + 2]),
        ]
    loads.append(pltpu.make_async_copy(w_rec_hbm, w_pair.at[core], local_sem.at[9]))
    for load in loads:
        load.start()

    arrivals, departures, background = {"w_rec": loads[9].wait}, [], []

    def bytes_of(ref, sem):
        return pltpu.make_async_copy(ref, ref, sem).wait

    def arrived(name):
        arrivals.pop(name)()

    def advance(count):
        for _ in range(count):
            background.pop(0)()

    def finish():
        advance(len(background))
        for name in list(arrivals):
            arrived(name)
        for departed in departures:
            departed()

    def exchanged(name, ref, peers, send_sem, recv_sem):
        part = ref.at[pl.ds(0, peers)]
        arrivals[name] = bytes_of(part, recv_sem)
        departures.append(bytes_of(part, send_sem))

    x, y = lax.rem(chip, SIDE), lax.div(chip, SIDE)

    def hops(shift, size):
        return min(shift, size - shift)

    shifts = sorted(
        ((dx, dy, dc) for dx in range(SIDE) for dy in range(SIDE) for dc in range(2)),
        key=lambda s: -(hops(s[0], SIDE) + hops(s[1], SIDE)),
    )
    plane = [
        (pop, 2 * (SIDE * lax.rem(y + dy, SIDE) + lax.rem(x + dx, SIDE)) + (1 - core if dc else core))
        for dx, dy, dc in shifts
        if dx + dy + dc > 0
    ]
    same_core = [dc == 0 for dx, dy, dc in shifts if dx + dy + dc > 0]
    column = [
        (lax.rem(pop + k, pops), me) for k in sorted(range(1, pops), key=lambda k: -hops(k, pops))
    ]

    barrier = pltpu.get_barrier_semaphore()
    for peer in column + plane:
        pl.semaphore_signal(barrier, inc=1, device_id=peer, device_id_type=MESH)

    def push(source, target, peers, send_sem, recv_sem, by_core=False):
        for n, peer in enumerate(peers):
            src = source
            if by_core:
                src = source.at[core if same_core[n] else 1 - core]
            pltpu.make_async_remote_copy(
                src_ref=src,
                dst_ref=target,
                send_sem=send_sem,
                recv_sem=recv_sem,
                device_id=peer,
                device_id_type=MESH,
            ).start()

    lane1 = lax.broadcasted_iota(jnp.int32, (1, 128), 1)
    here = lax.div(lane1, 32) == lax.rem(pop, 4)

    def placed(row):
        return jnp.where(here, jnp.concatenate([row, row, row, row], axis=1), 0.0)

    indices = idx_ref[...].astype(F32)
    meta[pop, 0:1, :] = placed(indices[0:1])
    meta[pop, 1:2, :] = placed(indices[1:2])
    meta[pop, 2:8, :] = jnp.zeros((6, 128), F32)

    loads[0].wait()
    spot = lax.broadcasted_iota(jnp.int32, (32, KTAB), 1).astype(F32)
    diagonal = lax.broadcasted_iota(jnp.int32, (32, 32), 0) == lax.broadcasted_iota(
        jnp.int32, (32, 32), 1
    )

    def picks(row):
        column = jnp.sum(jnp.where(diagonal, row, 0.0), axis=1, keepdims=True)
        return jnp.where(spot == column, 1.0, 0.0).astype(BF16)

    pick = jnp.concatenate([picks(indices[0:1]), picks(indices[1:2])], axis=0)
    picked = dot(pick, table_v[...]).astype(BF16)
    for half in range(2):
        rows_src[half, 0:16, :] = picked[16 * half : 16 * half + 16]
        rows_src[half, 16:32, :] = picked[32 + 16 * half : 48 + 16 * half]
    rows_v[me] = rows_src[core]
    tt_all[core, chip] = table_v[...].astype(F32).T.astype(BF16)

    drive = jnp.broadcast_to(bias_ref[...], (STEPS * EP, COLS))
    x_v[STEPS * EPIS :, :] = jnp.zeros((STEPS, NEUR), F32)
    for q, part in enumerate(parts):
        loads[2 * q + 1].wait()
        for e in range(EPIS):
            x_v[STEPS * e : STEPS * (e + 1), part] = spk_v[e, :, part].astype(F32)
        loads[2 * q + 2].wait()
        drive = drive + dot(x_v[:, part].astype(BF16), w_in_v[part, :])
    drive_v[...] = drive

    def drive_at(t):
        return drive_v[pl.ds(t, EP, stride=STEPS), :]

    drive0 = drive_at(0)
    drive1 = drive_at(1)
    pair_v[core, 0:16, :] = drive_at(2)
    pair_v[core, 16:32, :] = drive_at(3)
    pair_v[core, 32:40, :] = jnp.broadcast_to(leak_ref[...], (8, 128))
    pair_v[core, 40:48, :] = jnp.broadcast_to(readout_ref[...], (8, 128))
    spikes0 = squash(drive0)
    m1[me] = spikes0

    pl.semaphore_wait(barrier, TP - 1 + pops - 1)


    push(m1.at[me], m1.at[me], plane, m1_send, m1_recv)
    exchanged("m1", m1, TP - 1, m1_send, m1_recv)
    push(rows_src, rows_v.at[me], plane, rows_send, rows_recv, by_core=True)
    exchanged("rows", rows_v, TP - 1, rows_send, rows_recv)

    to_mate = [
        pltpu.make_async_remote_copy(
            src_ref=src,
            dst_ref=dst,
            send_sem=pair_send.at[i],
            recv_sem=pair_recv.at[i],
            device_id=(pop, mate),
            device_id_type=MESH,
        )
        for i, (src, dst) in enumerate(
            (
                (pair_v.at[core], pair_v.at[core]),
                (w_rec_hbm, w_pair.at[core]),
                (tt_all.at[core], tt_all.at[core]),
            )
        )
    ]
    def start_mate(i):
        to_mate[i].start()
        arrivals["mate%d" % i] = to_mate[i].wait_recv
        departures.append(to_mate[i].wait_send)

    start_mate(0)
    start_mate(1)

    first = lax.rem(chip, SIDE) * (1 - core) + lax.div(chip, SIDE) * core
    second = lax.div(chip, SIDE) * (1 - core) + lax.rem(chip, SIDE) * core

    def chip_at(u, v):
        return (u * (1 - core) + v * core) + SIDE * (v * (1 - core) + u * core)

    def step(w, by):
        return lax.rem(w + by, SIDE)

    across = [first, step(first, 3), step(first, 1), step(first, 2)]
    v_minus, v_plus, v_far = step(second, 3), step(second, 1), step(second, 2)

    def gather_ops(ref, start, low, total, send_sem, recv_sem):
        def part(slot, half):
            if half == 0:
                return ref.at[slot, pl.ds(start, low)]
            if half == 1:
                return ref.at[slot, pl.ds(start + low, total - low)]
            return ref.at[slot, pl.ds(start, total)]

        def send(slot, to, sem, half=None):
            pltpu.make_async_remote_copy(
                src_ref=part(slot, half),
                dst_ref=part(slot, half),
                send_sem=send_sem,
                recv_sem=recv_sem.at[sem],
                device_id=(pop, 2 * to + core),
                device_id_type=MESH,
            ).start()

        def wait(slot, sem, half=None):
            piece = part(slot, half)
            pltpu.make_async_copy(piece, piece, recv_sem.at[sem]).wait()

        def along(i):
            slot = chip_at(across[i], second)
            send(slot, chip_at(first, v_plus), 4 + 4 * i)
            send(slot, chip_at(first, v_minus), 5 + 4 * i)

        def near(i):
            slot = chip_at(across[i], second)
            wait(slot, i - 1)
            send(slot, chip_at(across[3 - i], second), 1 + i, half=i - 1)
            along(i)
            return slot

        def far():
            slot = chip_at(across[3], second)
            wait(slot, 2, half=0)
            wait(slot, 3, half=1)
            along(3)
            return slot

        def side_minus(i):
            slot = chip_at(across[i], v_minus)
            wait(slot, 4 + 4 * i)
            send(slot, chip_at(first, v_plus), 6 + 4 * i, half=0)
            return slot

        def side_plus(i):
            slot = chip_at(across[i], v_plus)
            wait(slot, 5 + 4 * i)
            send(slot, chip_at(first, v_minus), 7 + 4 * i, half=1)
            return slot

        def last(i):
            slot = chip_at(across[i], v_far)
            wait(slot, 6 + 4 * i, half=0)
            wait(slot, 7 + 4 * i, half=1)
            return slot

        def begin():
            slot = chip_at(first, second)
            send(slot, chip_at(across[2], second), 0)
            send(slot, chip_at(across[1], second), 1)
            along(0)

        return begin, near, far, side_minus, side_plus, last

    tt_ref = tt_all.at[core]
    tt_begin, tt_near, tt_far, tt_minus, tt_plus, tt_last = gather_ops(
        tt_ref, 0, 64, COLS, tt_send, tt_recv
    )
    tt_begin()
    departures.append(bytes_of(tt_ref.at[pl.ds(0, CHIPS - 1)], tt_send))
    background += [
        lambda: tt_near(1),
        lambda: tt_near(2),
        lambda: tt_minus(0),
        lambda: tt_plus(0),
        lambda: tt_far(),
        lambda: tt_minus(1),
        lambda: tt_plus(1),
        lambda: tt_minus(2),
        lambda: tt_plus(2),
        lambda: tt_minus(3),
        lambda: tt_plus(3),
        lambda: tt_last(0),
        lambda: tt_last(1),
        lambda: tt_last(2),
        lambda: tt_last(3),
        lambda: start_mate(2),
    ]

    if pops > 1:
        push(meta.at[pop], meta.at[pop], column, meta_send, meta_recv)
        exchanged("meta", meta, pops - 1, meta_send, meta_recv)

    arrived("w_rec")
    arrived("m1")

    def both(ref, c, low, high):
        return jnp.concatenate([ref[2 * c, low:high, :], ref[2 * c + 1, low:high, :]], axis=1)

    recurrent1 = jnp.zeros((16, COLS), F32)
    for c in range(CHIPS):
        recurrent1 = recurrent1 + dot(
            both(m1, c, 0, 16), w_pair[core, pl.ds(PAIR * c, PAIR), :]
        )
    m2[me] = leak_ref[...] * (drive0 - spikes0.astype(F32)) + (drive1 + recurrent1)

    push(m2.at[me], m2.at[me], plane, m2_send, m2_recv)
    exchanged("m2", m2, TP - 1, m2_send, m2_recv)

    advance(4)
    arrived("rows")
    project1 = jnp.zeros((HALF, EP), F32)
    for c in range(CHIPS):
        project1 = project1 + dot_nt(both(rows_v, c, 0, 16), both(m1, c, 0, 16))
    for e in range(EPIS):
        proj_v[e] = jnp.broadcast_to(sigma_scale * project1[:, e : e + 1], (HALF, 128))

    advance(1)

    arrived("mate0")
    arrived("mate1")
    arrived("m2")

    advance(4)
    acc_v[...] = jnp.zeros_like(acc_v)
    accp_v[...] = jnp.zeros_like(accp_v)

    def weights(c):
        rows = pl.ds(pl.multiple_of(PAIR * c, PAIR), PAIR)
        return jnp.concatenate([w_pair[0, rows, :], w_pair[1, rows, :]], axis=1)

    def spread(e):
        return jnp.concatenate([proj_v[e], proj_v[e]], axis=1)

    def step2(i, _):
        for k in range(2):
            c = 2 * i + k
            base = 2.0 * both(m2, c, 0, 16) - 2.0
            post = 2.0 * both(rows_v, c, 16, 32).astype(F32)
            for e in range(EPIS):
                lhs_v[k, HALF * e : HALF * (e + 1), :] = (
                    0.5 + 0.5 * jnp.tanh(base[e : e + 1] + spread(e) * post)
                ).astype(BF16)
        for k in range(2):
            c = 2 * i + k
            acc_v[...] += dot(lhs_v[k], weights(c))
            accp_v[...] += dot_nt(lhs_v[k], both(rows_v, c, 0, 16))
        return 0

    lax.fori_loop(0, CHIPS // 2, step2, 0)

    slot_of = lax.broadcasted_iota(jnp.int32, (KTAB, 128), 0).astype(F32)
    per_group = min(4, pops)

    def group_row(ref, g, row):
        total = ref[per_group * g, row : row + 1, :]
        for k in range(1, per_group):
            total = total + ref[per_group * g + k, row : row + 1, :]
        return total

    def choose_posts():
        if pops > 1:
            arrived("meta")
        for g in range(groups):
            chosen = jnp.where(slot_of == group_row(meta, g, 1), 1.0, 0.0)
            post_all[128 * g : 128 * (g + 1), :] = dot(
                chosen.T.astype(BF16), table_v[...]
            ).astype(BF16)

    leak = jnp.concatenate([pair_v[0, 32:33, :], pair_v[1, 32:33, :]], axis=1)
    readout = jnp.concatenate([pair_v[0, 40:41, :], pair_v[1, 40:41, :]], axis=1)
    drive2 = jnp.concatenate([pair_v[0, 0:16, :], pair_v[1, 0:16, :]], axis=1)
    drive3 = jnp.concatenate([pair_v[0, 16:32, :], pair_v[1, 16:32, :]], axis=1)
    post_here = both(rows_v, chip, 16, 32).astype(F32)
    base_here = both(m2, chip, 0, 16)
    eye = lax.broadcasted_iota(jnp.int32, (HALF, HALF), 0) == lax.broadcasted_iota(
        jnp.int32, (HALF, HALF), 1
    )

    def projection(e):
        square = accp_v[HALF * e : HALF * (e + 1), :]
        own = jnp.sum(jnp.where(eye, square, 0.0), axis=1, keepdims=True)
        return sigma_scale * own * post_here

    first_spikes = both(m1, chip, 0, 16).astype(F32)
    real = lax.broadcasted_iota(jnp.int32, (EP, PAIR), 0) < EPIS
    spike_sum = jnp.broadcast_to(
        jnp.sum(jnp.where(real, first_spikes, 0.0), axis=0, keepdims=True), (HALF, PAIR)
    )
    pieces = [
        gather_ops(spikes_v, PIECE * q, 48, PIECE, sp_send, sp_recv.at[q]) for q in range(PIECES)
    ]
    departures.append(bytes_of(spikes_v.at[pl.ds(0, CHIPS - 1)], sp_send))
    for e in range(EPIS):
        rows = slice(HALF * e, HALF * (e + 1))
        membrane1 = base_here[e : e + 1] + spread(e) * post_here
        spikes1 = squash(membrane1).astype(F32)
        membrane2 = leak * (membrane1 - spikes1) + (
            drive2[e : e + 1] + acc_v[rows, :] + projection(e)
        )
        spikes2 = squash(membrane2)
        spikes_v[chip, rows, :] = spikes2
        wide = spikes2.astype(F32)
        spike_sum = spike_sum + (spikes1 + wide)
        mem_v[rows, :] = leak * (membrane2 - wide) + drive3[e : e + 1]
        if (e + 1) * HALF % PIECE == 0:
            pieces[e * HALF // PIECE][0]()

    acc_v[...] = jnp.zeros_like(acc_v)
    accp_v[...] = jnp.zeros_like(accp_v)

    def take(c):
        block = spikes_v[c]
        acc_v[...] += dot(block, weights(c))
        accp_v[...] += dot_nt(block, both(rows_v, c, 0, 16))

    advance(2)
    take(chip)
    order = [(1, 1), (1, 2), (3, 0), (4, 0), (2, None), (3, 1), (4, 1), (3, 2), (4, 2), (5, 0), (3, 3)]
    order += [(4, 3), (5, 1), (5, 2), (5, 3)]
    events = sorted((i + 4 * q, q, op) for q in range(PIECES) for i, op in enumerate(order))
    for when, (_, q, (kind, which)) in enumerate(events):
        slot = pieces[q][kind]() if which is None else pieces[q][kind](which)
        if q == PIECES - 1:
            take(slot)
        if when == len(events) // 2:
            choose_posts()

    for e in range(EPIS):
        rows = slice(HALF * e, HALF * (e + 1))
        membrane3 = mem_v[rows, :] + (acc_v[rows, :] + projection(e))
        spike_sum = spike_sum + squash(membrane3).astype(F32)

    reward = jnp.sum(spike_sum * readout, axis=1, keepdims=True)
    lane16 = lax.broadcasted_iota(jnp.int32, (HALF, 128), 1)
    member16 = lax.broadcasted_iota(jnp.int32, (HALF, 128), 0)
    mine = lane16 == member16 + (lax.rem(pop, 4) * 32 + core * HALF)
    m3[me] = jnp.sum(jnp.where(mine, reward, 0.0), axis=0, keepdims=True)

    push(m3.at[me], m3.at[me], plane, m3_send, m3_recv)
    exchanged("m3", m3, TP - 1, m3_send, m3_recv)

    advance(5)

    arrived("m3")
    returns_row = jnp.sum(m3[...], axis=0) / (EPIS * STEPS)
    returns_ref[...] = (
        returns_row[:, 0:32] + returns_row[:, 32:64] + returns_row[:, 64:96] + returns_row[:, 96:128]
    )
    ranks = rank_ref[...].astype(F32) / (32 * pops - 1) - 0.5
    m4[pop] = placed(ranks) + returns_row

    if pops > 1:
        push(m4.at[pop], m4.at[pop], column, m4_send, m4_recv)
        exchanged("m4", m4, pops - 1, m4_send, m4_recv)
        arrived("m4")

    high, low = [], []
    for g in range(groups):
        scaled = jnp.where(slot_of == group_row(meta, g, 0), group_row(m4, g, 0), 0.0)
        top = scaled.astype(BF16)
        high.append(top)
        low.append((scaled - top.astype(F32)).astype(BF16))
    mixed = dot(jnp.concatenate(high, axis=1), post_all[...]) + dot(
        jnp.concatenate(low, axis=1), post_all[...]
    )
    mixed = mixed * jnp.sqrt(jnp.float32(12.0 / (32 * pops)))
    top = mixed.astype(BF16)
    split = jnp.concatenate([top, (mixed - top.astype(F32)).astype(BF16)], axis=1)

    arrived("mate2")

    for k in range(2):
        for q in range(4):
            block = tt_all[k, 4 * q : 4 * q + 4].reshape(4 * COLS, KTAB)
            both_parts = dot(block, split)
            rows = (both_parts[:, 0:COLS] + both_parts[:, COLS:PAIR]).astype(BF16)
            for n in range(4):
                start = PAIR * (4 * q + n) + COLS * k
                grad_ref[start : start + COLS, :] = rows[COLS * n : COLS * (n + 1)]

    finish()


def shards(
    in_spikes, w_in, w_rec, leak_rate, neuron_bias, readout, pert_table, pert_idx, member_ranks
):
    pops = lax.axis_size("pop")
    vmem = pl.BlockSpec(memory_space=pltpu.VMEM)
    hbm = pl.BlockSpec(memory_space=pltpu.HBM)
    dma = pltpu.SemaphoreType.DMA
    returns, grad_rec = pl.pallas_call(
        functools.partial(kernel, pops),
        out_shape=(
            jax.ShapeDtypeStruct((1, 32), F32),
            jax.ShapeDtypeStruct((NEUR, COLS), BF16),
        ),
        in_specs=[hbm, hbm, hbm, vmem, vmem, vmem, hbm, vmem, vmem],
        out_specs=(vmem, vmem),
        scratch_shapes=[
            pltpu.VMEM((EPIS, STEPS, NEUR), jnp.int32),
            pltpu.VMEM((NEUR, COLS), BF16),
            pltpu.VMEM((2, NEUR, COLS), BF16),
            pltpu.VMEM((STEPS * EP, NEUR), F32),
            pltpu.VMEM((STEPS * EP, COLS), F32),
            pltpu.VMEM((KTAB, COLS), BF16),
            pltpu.VMEM((2, CHIPS, COLS, KTAB), BF16),
            pltpu.VMEM((2, 32, COLS), BF16),
            pltpu.VMEM((TP, 32, COLS), BF16),
            pltpu.VMEM((TP, EP, COLS), BF16),
            pltpu.VMEM((TP, EP, COLS), F32),
            pltpu.VMEM((2, 48, COLS), F32),
            pltpu.VMEM((pops, 8, 128), F32),
            pltpu.VMEM((TP, 1, 128), F32),
            pltpu.VMEM((pops, 1, 128), F32),
            pltpu.VMEM((EPIS, HALF, 128), F32),
            pltpu.VMEM((2, ROWS, PAIR), BF16),
            pltpu.VMEM((ROWS, PAIR), F32),
            pltpu.VMEM((ROWS, HALF), F32),
            pltpu.VMEM((ROWS, PAIR), F32),
            pltpu.VMEM((CHIPS, ROWS, PAIR), BF16),
            pltpu.VMEM((128 * max(1, pops // 4), COLS), BF16),
            dma((10,)),
            dma,
            dma,
            dma,
            dma,
            dma,
            dma,
            dma,
            dma,
            dma,
            dma,
            dma,
            dma,
            dma((3,)),
            dma((3,)),
            dma,
            dma((20,)),
            dma,
            dma((PIECES, 20)),
        ],
        compiler_params=pltpu.CompilerParams(
            collective_id=0, has_side_effects=True, vmem_limit_bytes=60 * 1024 * 1024
        ),
        name="rollout",
    )(
        in_spikes.transpose(1, 0, 2),
        w_in,
        w_rec,
        leak_rate.reshape(1, COLS),
        neuron_bias.reshape(1, COLS),
        readout.reshape(1, COLS),
        pert_table,
        pert_idx.T,
        member_ranks.reshape(1, 32),
    )
    return returns.reshape(32), grad_rec


def solution(mesh):
    placed = (
        P(),
        P(None, "tp"),
        P(None, "tp"),
        P("tp"),
        P("tp"),
        P("tp"),
        P(None, "tp"),
        P("pop", None),
        P("pop"),
    )
    return jax.shard_map(
        shards, mesh=mesh, in_specs=placed, out_specs=(P("pop"), P(None, "tp")), check_vma=False
    )
```

```python
import functools

import jax
import jax.numpy as jnp
from jax import lax
from jax.experimental import pallas as pl
from jax.experimental.pallas import tpu as pltpu
from jax.sharding import PartitionSpec as P

MESH = pl.DeviceIdType.MESH
F32 = jnp.float32
BF16 = jnp.bfloat16
sigma_scale = 0.01

STEPS = 4
EPIS = 15
EP = 16
SIDE = 4
CHIPS = 16
TP = 32
COLS = 128
PAIR = 256
HALF = 16
ROWS = EPIS * HALF
PIECES = 3
PIECE = ROWS // PIECES
LOW = 48
NEUR = 4096
KTAB = 256

NT = (((1,), (1,)), ((), ()))
TN = (((0,), (0,)), ((), ()))


def dot(left, right):
    return jnp.dot(left, right, preferred_element_type=F32)


def dot_nt(left, right):
    return lax.dot_general(left, right, NT, preferred_element_type=F32)


def squash(membrane):
    return (0.5 + 0.5 * jnp.tanh(2.0 * membrane - 2.0)).astype(BF16)


def kernel(
    pops,
    in_hbm,
    w_in_hbm,
    w_rec_hbm,
    leak_ref,
    bias_ref,
    readout_ref,
    table_hbm,
    idx_ref,
    rank_ref,
    returns_ref,
    tt_all,
    split_ref,
    spk_v,
    w_in_v,
    w_pair,
    x_v,
    drive_v,
    table_v,
    rows_src,
    rows_v,
    m1,
    m2,
    pair_v,
    meta,
    m3,
    m4,
    proj_v,
    lhs_v,
    acc_v,
    accp_v,
    mem_v,
    spikes_v,
    post_all,
    local_sem,
    m1_send,
    m1_recv,
    rows_send,
    rows_recv,
    m2_send,
    m2_recv,
    m3_send,
    m3_recv,
    m4_send,
    m4_recv,
    meta_send,
    meta_recv,
    pair_send,
    pair_recv,
    tt_send,
    tt_recv,
    sp_send,
    sp_recv,
):
    pop = lax.axis_index("pop")
    me = lax.axis_index("tp")
    core = lax.rem(me, 2)
    chip = lax.div(me, 2)
    mate = me + 1 - 2 * core
    groups = max(1, pops // 4)
    quarter = NEUR // 4
    parts = [pl.ds(quarter * q, quarter) for q in range(4)]
    loads = [pltpu.make_async_copy(table_hbm, table_v, local_sem.at[0])]
    for q, part in enumerate(parts):
        loads += [
            pltpu.make_async_copy(
                in_hbm.at[:, :, part], spk_v.at[:, :, part], local_sem.at[2 * q + 1]
            ),
            pltpu.make_async_copy(w_in_hbm.at[part], w_in_v.at[part], local_sem.at[2 * q + 2]),
        ]
    loads.append(pltpu.make_async_copy(w_rec_hbm, w_pair.at[core], local_sem.at[9]))
    for load in loads:
        load.start()

    arrivals, departures, background = {"w_rec": loads[9].wait}, [], []

    def bytes_of(ref, sem):
        return pltpu.make_async_copy(ref, ref, sem).wait

    def arrived(name):
        arrivals.pop(name)()

    def advance(count):
        for _ in range(count):
            background.pop(0)()

    def finish():
        advance(len(background))
        for name in list(arrivals):
            arrived(name)
        for departed in departures:
            departed()

    def exchanged(name, ref, peers, send_sem, recv_sem):
        part = ref.at[pl.ds(0, peers)]
        arrivals[name] = bytes_of(part, recv_sem)
        departures.append(bytes_of(part, send_sem))

    x, y = lax.rem(chip, SIDE), lax.div(chip, SIDE)

    def hops(shift, size):
        return min(shift, size - shift)

    shifts = sorted(
        ((dx, dy, dc) for dx in range(SIDE) for dy in range(SIDE) for dc in range(2)),
        key=lambda s: -(hops(s[0], SIDE) + hops(s[1], SIDE)),
    )
    plane = [
        (pop, 2 * (SIDE * lax.rem(y + dy, SIDE) + lax.rem(x + dx, SIDE)) + (1 - core if dc else core))
        for dx, dy, dc in shifts
        if dx + dy + dc > 0
    ]
    same_core = [dc == 0 for dx, dy, dc in shifts if dx + dy + dc > 0]
    column = [
        (lax.rem(pop + k, pops), me) for k in sorted(range(1, pops), key=lambda k: -hops(k, pops))
    ]

    barrier = pltpu.get_barrier_semaphore()
    for peer in column + plane:
        pl.semaphore_signal(barrier, inc=1, device_id=peer, device_id_type=MESH)

    def push(source, target, peers, send_sem, recv_sem, by_core=False):
        for n, peer in enumerate(peers):
            src = source
            if by_core:
                src = source.at[core if same_core[n] else 1 - core]
            pltpu.make_async_remote_copy(
                src_ref=src,
                dst_ref=target,
                send_sem=send_sem,
                recv_sem=recv_sem,
                device_id=peer,
                device_id_type=MESH,
            ).start()

    lane1 = lax.broadcasted_iota(jnp.int32, (1, 128), 1)
    here = lax.div(lane1, 32) == lax.rem(pop, 4)

    def placed(row):
        return jnp.where(here, jnp.concatenate([row, row, row, row], axis=1), 0.0)

    indices = idx_ref[...].astype(F32)
    meta[pop, 0:1, :] = placed(indices[0:1])
    meta[pop, 1:2, :] = placed(indices[1:2])
    meta[pop, 2:8, :] = jnp.zeros((6, 128), F32)

    loads[0].wait()
    spot = lax.broadcasted_iota(jnp.int32, (32, KTAB), 1).astype(F32)
    diagonal = lax.broadcasted_iota(jnp.int32, (32, 32), 0) == lax.broadcasted_iota(
        jnp.int32, (32, 32), 1
    )

    def picks(row):
        column = jnp.sum(jnp.where(diagonal, row, 0.0), axis=1, keepdims=True)
        return jnp.where(spot == column, 1.0, 0.0).astype(BF16)

    pick = jnp.concatenate([picks(indices[0:1]), picks(indices[1:2])], axis=0)
    picked = dot(pick, table_v[...]).astype(BF16)
    for half in range(2):
        rows_src[half, 0:16, :] = picked[16 * half : 16 * half + 16]
        rows_src[half, 16:32, :] = picked[32 + 16 * half : 48 + 16 * half]
    rows_v[me] = rows_src[core]
    tt_all[core, chip] = table_v[...].astype(F32).T.astype(BF16)

    drive = jnp.broadcast_to(bias_ref[...], (STEPS * EP, COLS))
    x_v[STEPS * EPIS :, :] = jnp.zeros((STEPS, NEUR), F32)
    for q, part in enumerate(parts):
        loads[2 * q + 1].wait()
        for e in range(EPIS):
            x_v[STEPS * e : STEPS * (e + 1), part] = spk_v[e, :, part].astype(F32)
        loads[2 * q + 2].wait()
        drive = drive + dot(x_v[:, part].astype(BF16), w_in_v[part, :])
    drive_v[...] = drive

    def drive_at(t):
        return drive_v[pl.ds(t, EP, stride=STEPS), :]

    drive0 = drive_at(0)
    drive1 = drive_at(1)
    pair_v[core, 0:16, :] = drive_at(2)
    pair_v[core, 16:32, :] = drive_at(3)
    pair_v[core, 32:40, :] = jnp.broadcast_to(leak_ref[...], (8, 128))
    pair_v[core, 40:48, :] = jnp.broadcast_to(readout_ref[...], (8, 128))
    spikes0 = squash(drive0)
    m1[me] = spikes0

    pl.semaphore_wait(barrier, TP - 1 + pops - 1)


    push(m1.at[me], m1.at[me], plane, m1_send, m1_recv)
    exchanged("m1", m1, TP - 1, m1_send, m1_recv)
    push(rows_src, rows_v.at[me], plane, rows_send, rows_recv, by_core=True)
    exchanged("rows", rows_v, TP - 1, rows_send, rows_recv)

    to_mate = [
        pltpu.make_async_remote_copy(
            src_ref=src,
            dst_ref=dst,
            send_sem=pair_send.at[i],
            recv_sem=pair_recv.at[i],
            device_id=(pop, mate),
            device_id_type=MESH,
        )
        for i, (src, dst) in enumerate(
            (
                (pair_v.at[core], pair_v.at[core]),
                (w_rec_hbm, w_pair.at[core]),
            )
        )
    ]

    def start_mate(i):
        to_mate[i].start()
        arrivals["mate%d" % i] = to_mate[i].wait_recv
        departures.append(to_mate[i].wait_send)

    start_mate(0)
    start_mate(1)

    first = lax.rem(chip, SIDE) * (1 - core) + lax.div(chip, SIDE) * core
    second = lax.div(chip, SIDE) * (1 - core) + lax.rem(chip, SIDE) * core

    def chip_at(u, v):
        return (u * (1 - core) + v * core) + SIDE * (v * (1 - core) + u * core)

    def step(w, by):
        return lax.rem(w + by, SIDE)

    across = [first, step(first, 3), step(first, 1), step(first, 2)]
    v_minus, v_plus, v_far = step(second, 3), step(second, 1), step(second, 2)

    def gather_ops(ref, start, low, total, send_sem, recv_sem):
        def part(slot, half):
            if half == 0:
                return ref.at[slot, pl.ds(start, low)]
            if half == 1:
                return ref.at[slot, pl.ds(start + low, total - low)]
            return ref.at[slot, pl.ds(start, total)]

        def send(slot, to, sem, half=None):
            pltpu.make_async_remote_copy(
                src_ref=part(slot, half),
                dst_ref=part(slot, half),
                send_sem=send_sem,
                recv_sem=recv_sem.at[sem],
                device_id=(pop, 2 * to + core),
                device_id_type=MESH,
            ).start()

        def wait(slot, sem, half=None):
            piece = part(slot, half)
            pltpu.make_async_copy(piece, piece, recv_sem.at[sem]).wait()

        def along(i):
            slot = chip_at(across[i], second)
            send(slot, chip_at(first, v_plus), 4 + 4 * i)
            send(slot, chip_at(first, v_minus), 5 + 4 * i)

        def near(i, onward=True):
            slot = chip_at(across[i], second)
            wait(slot, i - 1)
            send(slot, chip_at(across[3 - i], second), 1 + i, half=i - 1)
            if onward:
                along(i)
            return slot

        def far(onward=True):
            slot = chip_at(across[3], second)
            wait(slot, 2, half=0)
            wait(slot, 3, half=1)
            if onward:
                along(3)
            return slot

        def side_minus(i):
            slot = chip_at(across[i], v_minus)
            wait(slot, 4 + 4 * i)
            send(slot, chip_at(first, v_plus), 6 + 4 * i, half=0)
            return slot

        def side_plus(i):
            slot = chip_at(across[i], v_plus)
            wait(slot, 5 + 4 * i)
            send(slot, chip_at(first, v_minus), 7 + 4 * i, half=1)
            return slot

        def last(i):
            slot = chip_at(across[i], v_far)
            wait(slot, 6 + 4 * i, half=0)
            wait(slot, 7 + 4 * i, half=1)
            return slot

        def begin(onward=True):
            slot = chip_at(first, second)
            send(slot, chip_at(across[2], second), 0)
            send(slot, chip_at(across[1], second), 1)
            if onward:
                along(0)

        return begin, near, far, side_minus, side_plus, last, along

    tt_ref = tt_all.at[core]
    tt_begin, tt_near, tt_far, tt_minus, tt_plus, tt_last, tt_along = gather_ops(
        tt_ref, 0, 64, COLS, tt_send, tt_recv
    )
    tt_begin(onward=False)
    departures.append(bytes_of(tt_ref.at[pl.ds(0, CHIPS - 1)], tt_send))
    departures.append(bytes_of(tt_ref, pair_send.at[2]))
    arrivals["mate2"] = bytes_of(tt_ref, pair_recv.at[2])

    def share(slot):
        pltpu.make_async_remote_copy(
            src_ref=tt_all.at[core, slot],
            dst_ref=tt_all.at[core, slot],
            send_sem=pair_send.at[2],
            recv_sem=pair_recv.at[2],
            device_id=(pop, mate),
            device_id_type=MESH,
        ).start()

    def tt_second():
        for i in range(SIDE):
            tt_along(i)
        for i in range(SIDE):
            share(chip_at(across[i], second))

    def tt_sides():
        for i in range(SIDE):
            share(tt_minus(i))
            share(tt_plus(i))

    def tt_rest():
        for i in range(SIDE):
            share(tt_last(i))

    background += [
        lambda: tt_near(1, onward=False),
        lambda: tt_near(2, onward=False),
        lambda: tt_far(onward=False),
        tt_second,
        tt_sides,
        tt_rest,
    ]

    if pops > 1:
        push(meta.at[pop], meta.at[pop], column, meta_send, meta_recv)
        exchanged("meta", meta, pops - 1, meta_send, meta_recv)

    arrived("w_rec")
    arrived("m1")

    def both(ref, c, low, high):
        return jnp.concatenate([ref[2 * c, low:high, :], ref[2 * c + 1, low:high, :]], axis=1)

    recurrent1 = jnp.zeros((16, COLS), F32)
    for c in range(CHIPS):
        recurrent1 = recurrent1 + dot(
            both(m1, c, 0, 16), w_pair[core, pl.ds(PAIR * c, PAIR), :]
        )
    m2[me] = leak_ref[...] * (drive0 - spikes0.astype(F32)) + (drive1 + recurrent1)

    push(m2.at[me], m2.at[me], plane, m2_send, m2_recv)
    exchanged("m2", m2, TP - 1, m2_send, m2_recv)

    advance(2)
    arrived("rows")
    project1 = jnp.zeros((HALF, EP), F32)
    for c in range(CHIPS):
        project1 = project1 + dot_nt(both(rows_v, c, 0, 16), both(m1, c, 0, 16))
    for e in range(EPIS):
        proj_v[e] = jnp.broadcast_to(sigma_scale * project1[:, e : e + 1], (HALF, 128))

    advance(1)

    arrived("mate0")
    arrived("mate1")
    arrived("m2")

    acc_v[...] = jnp.zeros_like(acc_v)
    accp_v[...] = jnp.zeros_like(accp_v)

    def weights(c):
        rows = pl.ds(pl.multiple_of(PAIR * c, PAIR), PAIR)
        return jnp.concatenate([w_pair[0, rows, :], w_pair[1, rows, :]], axis=1)

    def spread(e):
        return jnp.concatenate([proj_v[e], proj_v[e]], axis=1)

    def step2(i, _):
        for k in range(2):
            c = 2 * i + k
            base = 2.0 * both(m2, c, 0, 16) - 2.0
            post = 2.0 * both(rows_v, c, 16, 32).astype(F32)
            for e in range(EPIS):
                lhs_v[k, HALF * e : HALF * (e + 1), :] = (
                    0.5 + 0.5 * jnp.tanh(base[e : e + 1] + spread(e) * post)
                ).astype(BF16)
        for k in range(2):
            c = 2 * i + k
            acc_v[...] += dot(lhs_v[k], weights(c))
            accp_v[...] += dot_nt(lhs_v[k], both(rows_v, c, 0, 16))
        return 0

    lax.fori_loop(0, CHIPS // 2, step2, 0)

    slot_of = lax.broadcasted_iota(jnp.int32, (KTAB, 128), 0).astype(F32)
    per_group = min(4, pops)

    def group_row(ref, g, row):
        total = ref[per_group * g, row : row + 1, :]
        for k in range(1, per_group):
            total = total + ref[per_group * g + k, row : row + 1, :]
        return total

    def choose_posts():
        if pops > 1:
            arrived("meta")
        for g in range(groups):
            chosen = jnp.where(slot_of == group_row(meta, g, 1), 1.0, 0.0)
            post_all[128 * g : 128 * (g + 1), :] = dot(
                chosen.T.astype(BF16), table_v[...]
            ).astype(BF16)

    leak = jnp.concatenate([pair_v[0, 32:33, :], pair_v[1, 32:33, :]], axis=1)
    readout = jnp.concatenate([pair_v[0, 40:41, :], pair_v[1, 40:41, :]], axis=1)
    drive2 = jnp.concatenate([pair_v[0, 0:16, :], pair_v[1, 0:16, :]], axis=1)
    drive3 = jnp.concatenate([pair_v[0, 16:32, :], pair_v[1, 16:32, :]], axis=1)
    post_here = both(rows_v, chip, 16, 32).astype(F32)
    base_here = both(m2, chip, 0, 16)
    eye = lax.broadcasted_iota(jnp.int32, (HALF, HALF), 0) == lax.broadcasted_iota(
        jnp.int32, (HALF, HALF), 1
    )

    def projection(e):
        square = accp_v[HALF * e : HALF * (e + 1), :]
        own = jnp.sum(jnp.where(eye, square, 0.0), axis=1, keepdims=True)
        return sigma_scale * own * post_here

    first_spikes = both(m1, chip, 0, 16).astype(F32)
    real = lax.broadcasted_iota(jnp.int32, (EP, PAIR), 0) < EPIS
    spike_sum = jnp.broadcast_to(
        jnp.sum(jnp.where(real, first_spikes, 0.0), axis=0, keepdims=True), (HALF, PAIR)
    )
    pieces = [
        gather_ops(spikes_v, PIECE * q, LOW, PIECE, sp_send, sp_recv.at[q]) for q in range(PIECES)
    ]
    departures.append(bytes_of(spikes_v.at[pl.ds(0, CHIPS - 1)], sp_send))
    for e in range(EPIS):
        rows = slice(HALF * e, HALF * (e + 1))
        membrane1 = base_here[e : e + 1] + spread(e) * post_here
        spikes1 = squash(membrane1).astype(F32)
        membrane2 = leak * (membrane1 - spikes1) + (
            drive2[e : e + 1] + acc_v[rows, :] + projection(e)
        )
        spikes2 = squash(membrane2)
        spikes_v[chip, rows, :] = spikes2
        wide = spikes2.astype(F32)
        spike_sum = spike_sum + (spikes1 + wide)
        mem_v[rows, :] = leak * (membrane2 - wide) + drive3[e : e + 1]
        if (e + 1) * HALF % PIECE == 0:
            pieces[e * HALF // PIECE][0]()

    acc_v[...] = jnp.zeros_like(acc_v)
    accp_v[...] = jnp.zeros_like(accp_v)

    def take(c):
        block = spikes_v[c]
        acc_v[...] += dot(block, weights(c))
        accp_v[...] += dot_nt(block, both(rows_v, c, 0, 16))

    take(chip)
    order = [(1, 1), (1, 2), (3, 0), (4, 0), (2, None), (3, 1), (4, 1), (3, 2), (4, 2), (5, 0), (3, 3)]
    order += [(4, 3), (5, 1), (5, 2), (5, 3)]
    stage = [0] * 4 + [1] * 5 + [2] * 3 + [3] * 3
    events = sorted((stage[i], q, i) for q in range(PIECES) for i in range(len(order)))
    for when, (_, q, i) in enumerate(events):
        kind, which = order[i]
        slot = pieces[q][kind]() if which is None else pieces[q][kind](which)
        if q == PIECES - 1:
            take(slot)
        if when == len(events) // 2:
            choose_posts()

    for e in range(EPIS):
        rows = slice(HALF * e, HALF * (e + 1))
        membrane3 = mem_v[rows, :] + (acc_v[rows, :] + projection(e))
        spike_sum = spike_sum + squash(membrane3).astype(F32)

    reward = jnp.sum(spike_sum * readout, axis=1, keepdims=True)
    lane16 = lax.broadcasted_iota(jnp.int32, (HALF, 128), 1)
    member16 = lax.broadcasted_iota(jnp.int32, (HALF, 128), 0)
    mine = lane16 == member16 + (lax.rem(pop, 4) * 32 + core * HALF)
    m3[me] = jnp.sum(jnp.where(mine, reward, 0.0), axis=0, keepdims=True)

    push(m3.at[me], m3.at[me], plane, m3_send, m3_recv)
    exchanged("m3", m3, TP - 1, m3_send, m3_recv)

    advance(1)

    arrived("m3")
    returns_row = jnp.sum(m3[...], axis=0) / (EPIS * STEPS)
    returns_ref[...] = (
        returns_row[:, 0:32] + returns_row[:, 32:64] + returns_row[:, 64:96] + returns_row[:, 96:128]
    )
    ranks = rank_ref[...].astype(F32) / (32 * pops - 1) - 0.5
    m4[pop] = placed(ranks) + returns_row

    if pops > 1:
        push(m4.at[pop], m4.at[pop], column, m4_send, m4_recv)
        exchanged("m4", m4, pops - 1, m4_send, m4_recv)
    advance(2)
    if pops > 1:
        arrived("m4")

    high, low = [], []
    for g in range(groups):
        scaled = jnp.where(slot_of == group_row(meta, g, 0), group_row(m4, g, 0), 0.0)
        top = scaled.astype(BF16)
        high.append(top)
        low.append((scaled - top.astype(F32)).astype(BF16))
    mixed = dot(jnp.concatenate(high, axis=1), post_all[...]) + dot(
        jnp.concatenate(low, axis=1), post_all[...]
    )
    mixed = mixed * jnp.sqrt(jnp.float32(12.0 / (32 * pops)))
    top = mixed.astype(BF16)
    split_ref[...] = jnp.concatenate([top, (mixed - top.astype(F32)).astype(BF16)], axis=1)
    arrived("mate2")
    finish()


def gradient(returns_in, tt_ref, split_ref, returns_ref, grad_hbm, grad_v, sems):
    returns_ref[...] = returns_in[...]
    stores = []
    for q in range(CHIPS // 4):
        for k in range(2):
            block = tt_ref[k, 4 * q : 4 * q + 4].reshape(4 * COLS, KTAB)
            both_parts = dot(block, split_ref[...])
            rows = (both_parts[:, 0:COLS] + both_parts[:, COLS:PAIR]).astype(BF16)
            for n in range(4):
                start = PAIR * (4 * q + n) + COLS * k
                grad_v[start : start + COLS, :] = rows[COLS * n : COLS * (n + 1)]
        part = pl.ds(4 * PAIR * q, 4 * PAIR)
        stores.append(pltpu.make_async_copy(grad_v.at[part], grad_hbm.at[part], sems.at[q]))
        stores[-1].start()
    for store in stores:
        store.wait()


def shards(
    in_spikes, w_in, w_rec, leak_rate, neuron_bias, readout, pert_table, pert_idx, member_ranks
):
    pops = lax.axis_size("pop")
    vmem = pl.BlockSpec(memory_space=pltpu.VMEM)
    hbm = pl.BlockSpec(memory_space=pltpu.HBM)
    dma = pltpu.SemaphoreType.DMA
    returns, table_t, split = pl.pallas_call(
        functools.partial(kernel, pops),
        out_shape=(
            jax.ShapeDtypeStruct((1, 32), F32),
            jax.ShapeDtypeStruct((2, CHIPS, COLS, KTAB), BF16),
            jax.ShapeDtypeStruct((KTAB, PAIR), BF16),
        ),
        in_specs=[hbm, hbm, hbm, vmem, vmem, vmem, hbm, vmem, vmem],
        out_specs=(vmem, vmem, vmem),
        scratch_shapes=[
            pltpu.VMEM((EPIS, STEPS, NEUR), jnp.int32),
            pltpu.VMEM((NEUR, COLS), BF16),
            pltpu.VMEM((2, NEUR, COLS), BF16),
            pltpu.VMEM((STEPS * EP, NEUR), F32),
            pltpu.VMEM((STEPS * EP, COLS), F32),
            pltpu.VMEM((KTAB, COLS), BF16),
            pltpu.VMEM((2, 32, COLS), BF16),
            pltpu.VMEM((TP, 32, COLS), BF16),
            pltpu.VMEM((TP, EP, COLS), BF16),
            pltpu.VMEM((TP, EP, COLS), F32),
            pltpu.VMEM((2, 48, COLS), F32),
            pltpu.VMEM((pops, 8, 128), F32),
            pltpu.VMEM((TP, 1, 128), F32),
            pltpu.VMEM((pops, 1, 128), F32),
            pltpu.VMEM((EPIS, HALF, 128), F32),
            pltpu.VMEM((2, ROWS, PAIR), BF16),
            pltpu.VMEM((ROWS, PAIR), F32),
            pltpu.VMEM((ROWS, HALF), F32),
            pltpu.VMEM((ROWS, PAIR), F32),
            pltpu.VMEM((CHIPS, ROWS, PAIR), BF16),
            pltpu.VMEM((128 * max(1, pops // 4), COLS), BF16),
            dma((10,)),
            dma,
            dma,
            dma,
            dma,
            dma,
            dma,
            dma,
            dma,
            dma,
            dma,
            dma,
            dma,
            dma((3,)),
            dma((3,)),
            dma,
            dma((20,)),
            dma,
            dma((PIECES, 20)),
        ],
        compiler_params=pltpu.CompilerParams(
            collective_id=0, has_side_effects=True, vmem_limit_bytes=53 * 1024 * 1024
        ),
        name="rollout",
    )(
        in_spikes.transpose(1, 0, 2),
        w_in,
        w_rec,
        leak_rate.reshape(1, COLS),
        neuron_bias.reshape(1, COLS),
        readout.reshape(1, COLS),
        pert_table,
        pert_idx.T,
        member_ranks.reshape(1, 32),
    )
    returns, grad_rec = pl.pallas_call(
        gradient,
        out_shape=(
            jax.ShapeDtypeStruct((1, 32), F32),
            jax.ShapeDtypeStruct((NEUR, COLS), BF16),
        ),
        in_specs=[vmem, vmem, vmem],
        out_specs=(vmem, hbm),
        scratch_shapes=[pltpu.VMEM((NEUR, COLS), BF16), dma((CHIPS // 4,))],
        compiler_params=pltpu.CompilerParams(vmem_limit_bytes=20 * 1024 * 1024),
        name="gradient",
    )(returns, table_t, split)
    return returns.reshape(32), grad_rec


def solution(mesh):
    placed = (
        P(),
        P(None, "tp"),
        P(None, "tp"),
        P("tp"),
        P("tp"),
        P("tp"),
        P(None, "tp"),
        P("pop", None),
        P("pop"),
    )
    return jax.shard_map(
        shards, mesh=mesh, in_specs=placed, out_specs=(P("pop"), P(None, "tp")), check_vma=False
    )
```

```python
import functools

import jax
import jax.numpy as jnp
from jax import lax
from jax.experimental import pallas as pl
from jax.experimental.pallas import tpu as pltpu
from jax.sharding import PartitionSpec as P

MESH = pl.DeviceIdType.MESH
F32 = jnp.float32
BF16 = jnp.bfloat16
sigma_scale = 0.01

STEPS = 4
EPIS = 15
EP = 16
SIDE = 4
CHIPS = 16
TP = 32
COLS = 128
PAIR = 256
HALF = 16
ROWS = EPIS * HALF
PIECES = 3
PIECE = ROWS // PIECES
LOW = 48
NEUR = 4096
KTAB = 256

NT = (((1,), (1,)), ((), ()))
TN = (((0,), (0,)), ((), ()))


def dot(left, right):
    return jnp.dot(left, right, preferred_element_type=F32)


def dot_nt(left, right):
    return lax.dot_general(left, right, NT, preferred_element_type=F32)


def squash(membrane):
    return (0.5 + 0.5 * jnp.tanh(2.0 * membrane - 2.0)).astype(BF16)


def kernel(
    pops,
    in_hbm,
    w_in_hbm,
    w_rec_hbm,
    leak_hbm,
    bias_hbm,
    readout_hbm,
    table_hbm,
    idx_hbm,
    rank_hbm,
    returns_ref,
    tt_hbm,
    split_ref,
    leak_ref,
    bias_ref,
    readout_ref,
    idx_ref,
    rank_ref,
    tt_all,
    spk_v,
    w_in_v,
    w_pair,
    x_v,
    drive_v,
    table_v,
    rows_src,
    rows_v,
    m1,
    m2,
    pair_v,
    meta,
    m3,
    m4,
    proj_v,
    lhs_v,
    acc_v,
    accp_v,
    mem_v,
    spikes_v,
    post_all,
    local_sem,
    m1_send,
    m1_recv,
    rows_send,
    rows_recv,
    m2_send,
    m2_recv,
    m3_send,
    m3_recv,
    m4_send,
    m4_recv,
    meta_send,
    meta_recv,
    pair_send,
    pair_recv,
    tt_send,
    tt_recv,
    sp_send,
    sp_recv,
):
    pop = lax.axis_index("pop")
    me = lax.axis_index("tp")
    core = lax.rem(me, 2)
    chip = lax.div(me, 2)
    mate = me + 1 - 2 * core
    groups = max(1, pops // 4)
    quarter = NEUR // 4
    parts = [pl.ds(quarter * q, quarter) for q in range(4)]
    loads = [pltpu.make_async_copy(table_hbm, table_v, local_sem.at[0])]
    for q, part in enumerate(parts):
        loads += [
            pltpu.make_async_copy(
                in_hbm.at[:, :, part], spk_v.at[:, :, part], local_sem.at[2 * q + 1]
            ),
            pltpu.make_async_copy(w_in_hbm.at[part], w_in_v.at[part], local_sem.at[2 * q + 2]),
        ]
    loads.append(pltpu.make_async_copy(w_rec_hbm, w_pair.at[core], local_sem.at[9]))
    small = [
        pltpu.make_async_copy(src, dst, local_sem.at[10 + i])
        for i, (src, dst) in enumerate(
            (
                (idx_hbm, idx_ref),
                (leak_hbm, leak_ref),
                (bias_hbm, bias_ref),
                (readout_hbm, readout_ref),
                (rank_hbm, rank_ref),
            )
        )
    ]
    small[0].start()
    for load in loads + small[1:]:
        load.start()

    arrivals, departures, background = {"w_rec": loads[9].wait}, [], []

    def bytes_of(ref, sem):
        return pltpu.make_async_copy(ref, ref, sem).wait

    def arrived(name):
        arrivals.pop(name)()

    def advance(count):
        for _ in range(count):
            background.pop(0)()

    def finish():
        advance(len(background))
        for name in list(arrivals):
            arrived(name)
        for departed in departures:
            departed()

    def exchanged(name, ref, peers, send_sem, recv_sem):
        part = ref.at[pl.ds(0, peers)]
        arrivals[name] = bytes_of(part, recv_sem)
        departures.append(bytes_of(part, send_sem))

    x, y = lax.rem(chip, SIDE), lax.div(chip, SIDE)

    def hops(shift, size):
        return min(shift, size - shift)

    shifts = sorted(
        ((dx, dy, dc) for dx in range(SIDE) for dy in range(SIDE) for dc in range(2)),
        key=lambda s: -(hops(s[0], SIDE) + hops(s[1], SIDE)),
    )
    plane = [
        (pop, 2 * (SIDE * lax.rem(y + dy, SIDE) + lax.rem(x + dx, SIDE)) + (1 - core if dc else core))
        for dx, dy, dc in shifts
        if dx + dy + dc > 0
    ]
    same_core = [dc == 0 for dx, dy, dc in shifts if dx + dy + dc > 0]
    column = [
        (lax.rem(pop + k, pops), me) for k in sorted(range(1, pops), key=lambda k: -hops(k, pops))
    ]

    barrier = pltpu.get_barrier_semaphore()
    for peer in column + plane:
        pl.semaphore_signal(barrier, inc=1, device_id=peer, device_id_type=MESH)

    def push(source, target, peers, send_sem, recv_sem, by_core=False):
        for n, peer in enumerate(peers):
            src = source
            if by_core:
                src = source.at[core if same_core[n] else 1 - core]
            pltpu.make_async_remote_copy(
                src_ref=src,
                dst_ref=target,
                send_sem=send_sem,
                recv_sem=recv_sem,
                device_id=peer,
                device_id_type=MESH,
            ).start()

    lane1 = lax.broadcasted_iota(jnp.int32, (1, 128), 1)
    here = lax.div(lane1, 32) == lax.rem(pop, 4)

    def placed(row):
        return jnp.where(here, jnp.concatenate([row, row, row, row], axis=1), 0.0)

    small[0].wait()
    indices = idx_ref[...].astype(F32)
    meta[pop, 0:1, :] = placed(indices[0:1])
    meta[pop, 1:2, :] = placed(indices[1:2])
    meta[pop, 2:8, :] = jnp.zeros((6, 128), F32)

    loads[0].wait()
    spot = lax.broadcasted_iota(jnp.int32, (32, KTAB), 1).astype(F32)
    diagonal = lax.broadcasted_iota(jnp.int32, (32, 32), 0) == lax.broadcasted_iota(
        jnp.int32, (32, 32), 1
    )

    def picks(row):
        column = jnp.sum(jnp.where(diagonal, row, 0.0), axis=1, keepdims=True)
        return jnp.where(spot == column, 1.0, 0.0).astype(BF16)

    pick = jnp.concatenate([picks(indices[0:1]), picks(indices[1:2])], axis=0)
    picked = dot(pick, table_v[...]).astype(BF16)
    for half in range(2):
        rows_src[half, 0:16, :] = picked[16 * half : 16 * half + 16]
        rows_src[half, 16:32, :] = picked[32 + 16 * half : 48 + 16 * half]
    rows_v[me] = rows_src[core]
    tt_all[core, chip] = table_v[...].astype(F32).T.astype(BF16)

    for load in small[1:]:
        load.wait()
    drive = jnp.broadcast_to(bias_ref[...], (STEPS * EP, COLS))
    x_v[STEPS * EPIS :, :] = jnp.zeros((STEPS, NEUR), F32)
    for q, part in enumerate(parts):
        loads[2 * q + 1].wait()
        for e in range(EPIS):
            x_v[STEPS * e : STEPS * (e + 1), part] = spk_v[e, :, part].astype(F32)
        loads[2 * q + 2].wait()
        drive = drive + dot(x_v[:, part].astype(BF16), w_in_v[part, :])
    drive_v[...] = drive

    def drive_at(t):
        return drive_v[pl.ds(t, EP, stride=STEPS), :]

    drive0 = drive_at(0)
    drive1 = drive_at(1)
    pair_v[core, 0:16, :] = drive_at(2)
    pair_v[core, 16:32, :] = drive_at(3)
    pair_v[core, 32:40, :] = jnp.broadcast_to(leak_ref[...], (8, 128))
    pair_v[core, 40:48, :] = jnp.broadcast_to(readout_ref[...], (8, 128))
    spikes0 = squash(drive0)
    m1[me] = spikes0

    pl.semaphore_wait(barrier, TP - 1 + pops - 1)


    push(m1.at[me], m1.at[me], plane, m1_send, m1_recv)
    exchanged("m1", m1, TP - 1, m1_send, m1_recv)
    push(rows_src, rows_v.at[me], plane, rows_send, rows_recv, by_core=True)
    exchanged("rows", rows_v, TP - 1, rows_send, rows_recv)

    to_mate = [
        pltpu.make_async_remote_copy(
            src_ref=src,
            dst_ref=dst,
            send_sem=pair_send.at[i],
            recv_sem=pair_recv.at[i],
            device_id=(pop, mate),
            device_id_type=MESH,
        )
        for i, (src, dst) in enumerate(
            (
                (pair_v.at[core], pair_v.at[core]),
                (w_rec_hbm, w_pair.at[core]),
            )
        )
    ]

    def start_mate(i):
        to_mate[i].start()
        arrivals["mate%d" % i] = to_mate[i].wait_recv
        departures.append(to_mate[i].wait_send)

    start_mate(0)
    start_mate(1)

    first = lax.rem(chip, SIDE) * (1 - core) + lax.div(chip, SIDE) * core
    second = lax.div(chip, SIDE) * (1 - core) + lax.rem(chip, SIDE) * core

    def chip_at(u, v):
        return (u * (1 - core) + v * core) + SIDE * (v * (1 - core) + u * core)

    def step(w, by):
        return lax.rem(w + by, SIDE)

    across = [first, step(first, 3), step(first, 1), step(first, 2)]
    v_minus, v_plus, v_far = step(second, 3), step(second, 1), step(second, 2)

    def gather_ops(ref, start, low, total, send_sem, recv_sem):
        def part(slot, half):
            if half == 0:
                return ref.at[slot, pl.ds(start, low)]
            if half == 1:
                return ref.at[slot, pl.ds(start + low, total - low)]
            return ref.at[slot, pl.ds(start, total)]

        def send(slot, to, sem, half=None):
            pltpu.make_async_remote_copy(
                src_ref=part(slot, half),
                dst_ref=part(slot, half),
                send_sem=send_sem,
                recv_sem=recv_sem.at[sem],
                device_id=(pop, 2 * to + core),
                device_id_type=MESH,
            ).start()

        def wait(slot, sem, half=None):
            piece = part(slot, half)
            pltpu.make_async_copy(piece, piece, recv_sem.at[sem]).wait()

        def along(i):
            slot = chip_at(across[i], second)
            send(slot, chip_at(first, v_plus), 4 + 4 * i)
            send(slot, chip_at(first, v_minus), 5 + 4 * i)

        def near(i, onward=True):
            slot = chip_at(across[i], second)
            wait(slot, i - 1)
            send(slot, chip_at(across[3 - i], second), 1 + i, half=i - 1)
            if onward:
                along(i)
            return slot

        def far(onward=True):
            slot = chip_at(across[3], second)
            wait(slot, 2, half=0)
            wait(slot, 3, half=1)
            if onward:
                along(3)
            return slot

        def side_minus(i):
            slot = chip_at(across[i], v_minus)
            wait(slot, 4 + 4 * i)
            send(slot, chip_at(first, v_plus), 6 + 4 * i, half=0)
            return slot

        def side_plus(i):
            slot = chip_at(across[i], v_plus)
            wait(slot, 5 + 4 * i)
            send(slot, chip_at(first, v_minus), 7 + 4 * i, half=1)
            return slot

        def last(i):
            slot = chip_at(across[i], v_far)
            wait(slot, 6 + 4 * i, half=0)
            wait(slot, 7 + 4 * i, half=1)
            return slot

        def begin(onward=True):
            slot = chip_at(first, second)
            send(slot, chip_at(across[2], second), 0)
            send(slot, chip_at(across[1], second), 1)
            if onward:
                along(0)

        return begin, near, far, side_minus, side_plus, last, along

    tt_ref = tt_all.at[core]
    tt_begin, tt_near, tt_far, tt_minus, tt_plus, tt_last, tt_along = gather_ops(
        tt_ref, 0, 64, COLS, tt_send, tt_recv
    )
    tt_begin(onward=False)
    departures.append(bytes_of(tt_ref.at[pl.ds(0, CHIPS - 1)], tt_send))
    departures.append(bytes_of(tt_ref, pair_send.at[2]))
    arrivals["mate2"] = bytes_of(tt_ref, pair_recv.at[2])

    def share(slot):
        pltpu.make_async_remote_copy(
            src_ref=tt_all.at[core, slot],
            dst_ref=tt_all.at[core, slot],
            send_sem=pair_send.at[2],
            recv_sem=pair_recv.at[2],
            device_id=(pop, mate),
            device_id_type=MESH,
        ).start()

    def tt_second():
        for i in range(SIDE):
            tt_along(i)
        for i in range(SIDE):
            share(chip_at(across[i], second))

    def tt_sides():
        for i in range(SIDE):
            share(tt_minus(i))
            share(tt_plus(i))

    def tt_rest():
        for i in range(SIDE):
            share(tt_last(i))

    background += [
        lambda: tt_near(1, onward=False),
        lambda: tt_near(2, onward=False),
        lambda: tt_far(onward=False),
        tt_second,
        tt_sides,
        tt_rest,
    ]

    if pops > 1:
        push(meta.at[pop], meta.at[pop], column, meta_send, meta_recv)
        exchanged("meta", meta, pops - 1, meta_send, meta_recv)

    arrived("w_rec")
    arrived("m1")

    def both(ref, c, low, high):
        return jnp.concatenate([ref[2 * c, low:high, :], ref[2 * c + 1, low:high, :]], axis=1)

    recurrent1 = jnp.zeros((16, COLS), F32)
    for c in range(CHIPS):
        recurrent1 = recurrent1 + dot(
            both(m1, c, 0, 16), w_pair[core, pl.ds(PAIR * c, PAIR), :]
        )
    m2[me] = leak_ref[...] * (drive0 - spikes0.astype(F32)) + (drive1 + recurrent1)

    push(m2.at[me], m2.at[me], plane, m2_send, m2_recv)
    exchanged("m2", m2, TP - 1, m2_send, m2_recv)

    advance(2)
    arrived("rows")
    project1 = jnp.zeros((HALF, EP), F32)
    for c in range(CHIPS):
        project1 = project1 + dot_nt(both(rows_v, c, 0, 16), both(m1, c, 0, 16))
    for e in range(EPIS):
        proj_v[e] = jnp.broadcast_to(sigma_scale * project1[:, e : e + 1], (HALF, 128))

    advance(1)

    arrived("mate0")
    arrived("mate1")
    arrived("m2")

    acc_v[...] = jnp.zeros_like(acc_v)
    accp_v[...] = jnp.zeros_like(accp_v)

    def weights(c):
        rows = pl.ds(pl.multiple_of(PAIR * c, PAIR), PAIR)
        return jnp.concatenate([w_pair[0, rows, :], w_pair[1, rows, :]], axis=1)

    def spread(e):
        return jnp.concatenate([proj_v[e], proj_v[e]], axis=1)

    def step2(i, _):
        for k in range(2):
            c = 2 * i + k
            base = 2.0 * both(m2, c, 0, 16) - 2.0
            post = 2.0 * both(rows_v, c, 16, 32).astype(F32)
            for e in range(EPIS):
                lhs_v[k, HALF * e : HALF * (e + 1), :] = (
                    0.5 + 0.5 * jnp.tanh(base[e : e + 1] + spread(e) * post)
                ).astype(BF16)
        for k in range(2):
            c = 2 * i + k
            acc_v[...] += dot(lhs_v[k], weights(c))
            accp_v[...] += dot_nt(lhs_v[k], both(rows_v, c, 0, 16))
        return 0

    lax.fori_loop(0, CHIPS // 2, step2, 0)

    slot_of = lax.broadcasted_iota(jnp.int32, (KTAB, 128), 0).astype(F32)
    per_group = min(4, pops)

    def group_row(ref, g, row):
        total = ref[per_group * g, row : row + 1, :]
        for k in range(1, per_group):
            total = total + ref[per_group * g + k, row : row + 1, :]
        return total

    def choose_posts():
        if pops > 1:
            arrived("meta")
        for g in range(groups):
            chosen = jnp.where(slot_of == group_row(meta, g, 1), 1.0, 0.0)
            post_all[128 * g : 128 * (g + 1), :] = dot(
                chosen.T.astype(BF16), table_v[...]
            ).astype(BF16)

    leak = jnp.concatenate([pair_v[0, 32:33, :], pair_v[1, 32:33, :]], axis=1)
    readout = jnp.concatenate([pair_v[0, 40:41, :], pair_v[1, 40:41, :]], axis=1)
    drive2 = jnp.concatenate([pair_v[0, 0:16, :], pair_v[1, 0:16, :]], axis=1)
    drive3 = jnp.concatenate([pair_v[0, 16:32, :], pair_v[1, 16:32, :]], axis=1)
    post_here = both(rows_v, chip, 16, 32).astype(F32)
    base_here = both(m2, chip, 0, 16)
    eye = lax.broadcasted_iota(jnp.int32, (HALF, HALF), 0) == lax.broadcasted_iota(
        jnp.int32, (HALF, HALF), 1
    )

    def projection(e):
        square = accp_v[HALF * e : HALF * (e + 1), :]
        own = jnp.sum(jnp.where(eye, square, 0.0), axis=1, keepdims=True)
        return sigma_scale * own * post_here

    first_spikes = both(m1, chip, 0, 16).astype(F32)
    real = lax.broadcasted_iota(jnp.int32, (EP, PAIR), 0) < EPIS
    spike_sum = jnp.broadcast_to(
        jnp.sum(jnp.where(real, first_spikes, 0.0), axis=0, keepdims=True), (HALF, PAIR)
    )
    pieces = [
        gather_ops(spikes_v, PIECE * q, LOW, PIECE, sp_send, sp_recv.at[q]) for q in range(PIECES)
    ]
    departures.append(bytes_of(spikes_v.at[pl.ds(0, CHIPS - 1)], sp_send))
    for e in range(EPIS):
        rows = slice(HALF * e, HALF * (e + 1))
        membrane1 = base_here[e : e + 1] + spread(e) * post_here
        spikes1 = squash(membrane1).astype(F32)
        membrane2 = leak * (membrane1 - spikes1) + (
            drive2[e : e + 1] + acc_v[rows, :] + projection(e)
        )
        spikes2 = squash(membrane2)
        spikes_v[chip, rows, :] = spikes2
        wide = spikes2.astype(F32)
        spike_sum = spike_sum + (spikes1 + wide)
        mem_v[rows, :] = leak * (membrane2 - wide) + drive3[e : e + 1]
        if (e + 1) * HALF % PIECE == 0:
            pieces[e * HALF // PIECE][0]()

    acc_v[...] = jnp.zeros_like(acc_v)
    accp_v[...] = jnp.zeros_like(accp_v)

    def take(c):
        block = spikes_v[c]
        acc_v[...] += dot(block, weights(c))
        accp_v[...] += dot_nt(block, both(rows_v, c, 0, 16))

    take(chip)
    order = [(1, 1), (1, 2), (3, 0), (4, 0), (2, None), (3, 1), (4, 1), (3, 2), (4, 2), (5, 0), (3, 3)]
    order += [(4, 3), (5, 1), (5, 2), (5, 3)]
    stage = [0] * 4 + [1] * 5 + [2] * 3 + [3] * 3
    events = sorted((stage[i], q, i) for q in range(PIECES) for i in range(len(order)))
    for when, (_, q, i) in enumerate(events):
        kind, which = order[i]
        slot = pieces[q][kind]() if which is None else pieces[q][kind](which)
        if q == PIECES - 1:
            take(slot)
        if when == len(events) // 2:
            choose_posts()

    for e in range(EPIS):
        rows = slice(HALF * e, HALF * (e + 1))
        membrane3 = mem_v[rows, :] + (acc_v[rows, :] + projection(e))
        spike_sum = spike_sum + squash(membrane3).astype(F32)

    reward = jnp.sum(spike_sum * readout, axis=1, keepdims=True)
    lane16 = lax.broadcasted_iota(jnp.int32, (HALF, 128), 1)
    member16 = lax.broadcasted_iota(jnp.int32, (HALF, 128), 0)
    mine = lane16 == member16 + (lax.rem(pop, 4) * 32 + core * HALF)
    m3[me] = jnp.sum(jnp.where(mine, reward, 0.0), axis=0, keepdims=True)

    push(m3.at[me], m3.at[me], plane, m3_send, m3_recv)
    exchanged("m3", m3, TP - 1, m3_send, m3_recv)

    advance(1)

    arrived("m3")
    returns_row = jnp.sum(m3[...], axis=0) / (EPIS * STEPS)
    returns_ref[...] = (
        returns_row[:, 0:32] + returns_row[:, 32:64] + returns_row[:, 64:96] + returns_row[:, 96:128]
    )
    ranks = rank_ref[...].astype(F32) / (32 * pops - 1) - 0.5
    m4[pop] = placed(ranks) + returns_row

    if pops > 1:
        push(m4.at[pop], m4.at[pop], column, m4_send, m4_recv)
        exchanged("m4", m4, pops - 1, m4_send, m4_recv)
    advance(2)
    saves = [
        pltpu.make_async_copy(tt_all.at[part], tt_hbm.at[part], local_sem.at[15 + i])
        for i, part in enumerate((core, 1 - core))
    ]
    saves[0].start()
    arrived("mate2")
    saves[1].start()
    if pops > 1:
        arrived("m4")

    high, low = [], []
    for g in range(groups):
        scaled = jnp.where(slot_of == group_row(meta, g, 0), group_row(m4, g, 0), 0.0)
        top = scaled.astype(BF16)
        high.append(top)
        low.append((scaled - top.astype(F32)).astype(BF16))
    mixed = dot(jnp.concatenate(high, axis=1), post_all[...]) + dot(
        jnp.concatenate(low, axis=1), post_all[...]
    )
    mixed = mixed * jnp.sqrt(jnp.float32(12.0 / (32 * pops)))
    top = mixed.astype(BF16)
    split_ref[...] = jnp.concatenate([top, (mixed - top.astype(F32)).astype(BF16)], axis=1)
    for save in saves:
        save.wait()
    finish()


def gradient(returns_in, tt_hbm, split_ref, returns_ref, grad_hbm, tt_v, grad_v, in_sems, out_sems):
    blocks = CHIPS // 4
    loads = [
        pltpu.make_async_copy(
            tt_hbm.at[:, pl.ds(4 * q, 4)], tt_v.at[:, pl.ds(4 * q, 4)], in_sems.at[q]
        )
        for q in range(blocks)
    ]
    for load in loads:
        load.start()
    returns_ref[...] = returns_in[...]
    stores = []
    for q in range(blocks):
        loads[q].wait()
        for k in range(2):
            block = tt_v[k, 4 * q : 4 * q + 4].reshape(4 * COLS, KTAB)
            both_parts = dot(block, split_ref[...])
            rows = (both_parts[:, 0:COLS] + both_parts[:, COLS:PAIR]).astype(BF16)
            for n in range(4):
                start = PAIR * (4 * q + n) + COLS * k
                grad_v[start : start + COLS, :] = rows[COLS * n : COLS * (n + 1)]
        part = pl.ds(4 * PAIR * q, 4 * PAIR)
        stores.append(pltpu.make_async_copy(grad_v.at[part], grad_hbm.at[part], out_sems.at[q]))
        stores[-1].start()
    for store in stores:
        store.wait()


def shards(
    in_spikes, w_in, w_rec, leak_rate, neuron_bias, readout, pert_table, pert_idx, member_ranks
):
    pops = lax.axis_size("pop")
    vmem = pl.BlockSpec(memory_space=pltpu.VMEM)
    hbm = pl.BlockSpec(memory_space=pltpu.HBM)
    dma = pltpu.SemaphoreType.DMA
    returns, table_t, split = pl.pallas_call(
        functools.partial(kernel, pops),
        out_shape=(
            jax.ShapeDtypeStruct((1, 32), F32),
            jax.ShapeDtypeStruct((2, CHIPS, COLS, KTAB), BF16),
            jax.ShapeDtypeStruct((KTAB, PAIR), BF16),
        ),
        in_specs=[hbm] * 9,
        out_specs=(vmem, hbm, vmem),
        scratch_shapes=[
            pltpu.VMEM((1, COLS), F32),
            pltpu.VMEM((1, COLS), F32),
            pltpu.VMEM((1, COLS), F32),
            pltpu.VMEM((2, 32), jnp.int32),
            pltpu.VMEM((1, 32), jnp.int32),
            pltpu.VMEM((2, CHIPS, COLS, KTAB), BF16),
            pltpu.VMEM((EPIS, STEPS, NEUR), jnp.int32),
            pltpu.VMEM((NEUR, COLS), BF16),
            pltpu.VMEM((2, NEUR, COLS), BF16),
            pltpu.VMEM((STEPS * EP, NEUR), F32),
            pltpu.VMEM((STEPS * EP, COLS), F32),
            pltpu.VMEM((KTAB, COLS), BF16),
            pltpu.VMEM((2, 32, COLS), BF16),
            pltpu.VMEM((TP, 32, COLS), BF16),
            pltpu.VMEM((TP, EP, COLS), BF16),
            pltpu.VMEM((TP, EP, COLS), F32),
            pltpu.VMEM((2, 48, COLS), F32),
            pltpu.VMEM((pops, 8, 128), F32),
            pltpu.VMEM((TP, 1, 128), F32),
            pltpu.VMEM((pops, 1, 128), F32),
            pltpu.VMEM((EPIS, HALF, 128), F32),
            pltpu.VMEM((2, ROWS, PAIR), BF16),
            pltpu.VMEM((ROWS, PAIR), F32),
            pltpu.VMEM((ROWS, HALF), F32),
            pltpu.VMEM((ROWS, PAIR), F32),
            pltpu.VMEM((CHIPS, ROWS, PAIR), BF16),
            pltpu.VMEM((128 * max(1, pops // 4), COLS), BF16),
            dma((17,)),
            dma,
            dma,
            dma,
            dma,
            dma,
            dma,
            dma,
            dma,
            dma,
            dma,
            dma,
            dma,
            dma((3,)),
            dma((3,)),
            dma,
            dma((20,)),
            dma,
            dma((PIECES, 20)),
        ],
        compiler_params=pltpu.CompilerParams(
            collective_id=0, has_side_effects=True, vmem_limit_bytes=60 * 1024 * 1024
        ),
        name="rollout",
    )(
        in_spikes.transpose(1, 0, 2),
        w_in,
        w_rec,
        leak_rate.reshape(1, COLS),
        neuron_bias.reshape(1, COLS),
        readout.reshape(1, COLS),
        pert_table,
        pert_idx.T,
        member_ranks.reshape(1, 32),
    )
    returns, grad_rec = pl.pallas_call(
        gradient,
        out_shape=(
            jax.ShapeDtypeStruct((1, 32), F32),
            jax.ShapeDtypeStruct((NEUR, COLS), BF16),
        ),
        in_specs=[vmem, hbm, vmem],
        out_specs=(vmem, hbm),
        scratch_shapes=[
            pltpu.VMEM((2, CHIPS, COLS, KTAB), BF16),
            pltpu.VMEM((NEUR, COLS), BF16),
            dma((CHIPS // 4,)),
            dma((CHIPS // 4,)),
        ],
        compiler_params=pltpu.CompilerParams(vmem_limit_bytes=60 * 1024 * 1024),
        name="gradient",
    )(returns, table_t, split)
    return returns.reshape(32), grad_rec


def solution(mesh):
    placed = (
        P(),
        P(None, "tp"),
        P(None, "tp"),
        P("tp"),
        P("tp"),
        P("tp"),
        P(None, "tp"),
        P("pop", None),
        P("pop"),
    )
    return jax.shard_map(
        shards, mesh=mesh, in_specs=placed, out_specs=(P("pop"), P(None, "tp")), check_vma=False
    )
```

```python
import functools

import jax
import jax.numpy as jnp
from jax import lax
from jax.experimental import pallas as pl
from jax.experimental.pallas import tpu as pltpu
from jax.sharding import PartitionSpec as P

MESH = pl.DeviceIdType.MESH
F32 = jnp.float32
BF16 = jnp.bfloat16
sigma_scale = 0.01

STEPS = 4
EPIS = 15
EP = 16
SIDE = 4
CHIPS = 16
TP = 32
COLS = 128
PAIR = 256
HALF = 16
ROWS = EPIS * HALF
PIECES = 3
PIECE = ROWS // PIECES
LOW = 48
NEUR = 4096
KTAB = 256

NT = (((1,), (1,)), ((), ()))
TN = (((0,), (0,)), ((), ()))


def dot(left, right):
    return jnp.dot(left, right, preferred_element_type=F32)


def dot_nt(left, right):
    return lax.dot_general(left, right, NT, preferred_element_type=F32)


def squash(membrane):
    return (0.5 + 0.5 * jnp.tanh(2.0 * membrane - 2.0)).astype(BF16)


def kernel(
    pops,
    in_hbm,
    w_in_hbm,
    w_rec_hbm,
    leak_hbm,
    bias_hbm,
    readout_hbm,
    table_hbm,
    idx_hbm,
    rank_hbm,
    returns_hbm,
    tt_hbm,
    split_hbm,
    returns_ref,
    split_ref,
    leak_ref,
    bias_ref,
    readout_ref,
    idx_ref,
    rank_ref,
    tt_all,
    spk_v,
    w_in_v,
    w_pair,
    x_v,
    drive_v,
    table_v,
    rows_src,
    rows_v,
    m1,
    m2,
    pair_v,
    meta,
    m3,
    m4,
    proj_v,
    lhs_v,
    acc_v,
    accp_v,
    mem_v,
    spikes_v,
    post_all,
    local_sem,
    m1_send,
    m1_recv,
    rows_send,
    rows_recv,
    m2_send,
    m2_recv,
    m3_send,
    m3_recv,
    m4_send,
    m4_recv,
    meta_send,
    meta_recv,
    pair_send,
    pair_recv,
    tt_send,
    tt_recv,
    sp_send,
    sp_recv,
):
    pop = lax.axis_index("pop")
    me = lax.axis_index("tp")
    core = lax.rem(me, 2)
    chip = lax.div(me, 2)
    mate = me + 1 - 2 * core
    groups = max(1, pops // 4)
    quarter = NEUR // 4
    parts = [pl.ds(quarter * q, quarter) for q in range(4)]
    loads = [pltpu.make_async_copy(table_hbm, table_v, local_sem.at[0])]
    for q, part in enumerate(parts):
        loads += [
            pltpu.make_async_copy(
                in_hbm.at[:, :, part], spk_v.at[:, :, part], local_sem.at[2 * q + 1]
            ),
            pltpu.make_async_copy(w_in_hbm.at[part], w_in_v.at[part], local_sem.at[2 * q + 2]),
        ]
    loads.append(pltpu.make_async_copy(w_rec_hbm, w_pair.at[core], local_sem.at[9]))
    small = [
        pltpu.make_async_copy(src, dst, local_sem.at[10 + i])
        for i, (src, dst) in enumerate(
            (
                (idx_hbm, idx_ref),
                (leak_hbm, leak_ref),
                (bias_hbm, bias_ref),
                (readout_hbm, readout_ref),
                (rank_hbm, rank_ref),
            )
        )
    ]
    small[0].start()
    for load in loads + small[1:]:
        load.start()

    arrivals, departures, background = {"w_rec": loads[9].wait}, [], []

    def bytes_of(ref, sem):
        return pltpu.make_async_copy(ref, ref, sem).wait

    def arrived(name):
        arrivals.pop(name)()

    def advance(count):
        for _ in range(count):
            background.pop(0)()

    def finish():
        advance(len(background))
        for name in list(arrivals):
            arrived(name)
        for departed in departures:
            departed()

    def exchanged(name, ref, peers, send_sem, recv_sem):
        part = ref.at[pl.ds(0, peers)]
        arrivals[name] = bytes_of(part, recv_sem)
        departures.append(bytes_of(part, send_sem))

    x, y = lax.rem(chip, SIDE), lax.div(chip, SIDE)

    def hops(shift, size):
        return min(shift, size - shift)

    shifts = sorted(
        ((dx, dy, dc) for dx in range(SIDE) for dy in range(SIDE) for dc in range(2)),
        key=lambda s: -(hops(s[0], SIDE) + hops(s[1], SIDE)),
    )
    plane = [
        (pop, 2 * (SIDE * lax.rem(y + dy, SIDE) + lax.rem(x + dx, SIDE)) + (1 - core if dc else core))
        for dx, dy, dc in shifts
        if dx + dy + dc > 0
    ]
    same_core = [dc == 0 for dx, dy, dc in shifts if dx + dy + dc > 0]
    column = [
        (lax.rem(pop + k, pops), me) for k in sorted(range(1, pops), key=lambda k: -hops(k, pops))
    ]

    barrier = pltpu.get_barrier_semaphore()
    for peer in column + plane:
        pl.semaphore_signal(barrier, inc=1, device_id=peer, device_id_type=MESH)

    def push(source, target, peers, send_sem, recv_sem, by_core=False):
        for n, peer in enumerate(peers):
            src = source
            if by_core:
                src = source.at[core if same_core[n] else 1 - core]
            pltpu.make_async_remote_copy(
                src_ref=src,
                dst_ref=target,
                send_sem=send_sem,
                recv_sem=recv_sem,
                device_id=peer,
                device_id_type=MESH,
            ).start()

    lane1 = lax.broadcasted_iota(jnp.int32, (1, 128), 1)
    here = lax.div(lane1, 32) == lax.rem(pop, 4)

    def placed(row):
        return jnp.where(here, jnp.concatenate([row, row, row, row], axis=1), 0.0)

    small[0].wait()
    indices = idx_ref[...].astype(F32)
    meta[pop, 0:1, :] = placed(indices[0:1])
    meta[pop, 1:2, :] = placed(indices[1:2])
    meta[pop, 2:8, :] = jnp.zeros((6, 128), F32)

    loads[0].wait()
    spot = lax.broadcasted_iota(jnp.int32, (32, KTAB), 1).astype(F32)
    diagonal = lax.broadcasted_iota(jnp.int32, (32, 32), 0) == lax.broadcasted_iota(
        jnp.int32, (32, 32), 1
    )

    def picks(row):
        column = jnp.sum(jnp.where(diagonal, row, 0.0), axis=1, keepdims=True)
        return jnp.where(spot == column, 1.0, 0.0).astype(BF16)

    pick = jnp.concatenate([picks(indices[0:1]), picks(indices[1:2])], axis=0)
    picked = dot(pick, table_v[...]).astype(BF16)
    for half in range(2):
        rows_src[half, 0:16, :] = picked[16 * half : 16 * half + 16]
        rows_src[half, 16:32, :] = picked[32 + 16 * half : 48 + 16 * half]
    rows_v[me] = rows_src[core]
    tt_all[core, chip] = table_v[...].astype(F32).T.astype(BF16)

    for load in small[1:]:
        load.wait()
    drive = jnp.broadcast_to(bias_ref[...], (STEPS * EP, COLS))
    x_v[STEPS * EPIS :, :] = jnp.zeros((STEPS, NEUR), F32)
    for q, part in enumerate(parts):
        loads[2 * q + 1].wait()
        for e in range(EPIS):
            x_v[STEPS * e : STEPS * (e + 1), part] = spk_v[e, :, part].astype(F32)
        loads[2 * q + 2].wait()
        drive = drive + dot(x_v[:, part].astype(BF16), w_in_v[part, :])
    drive_v[...] = drive

    def drive_at(t):
        return drive_v[pl.ds(t, EP, stride=STEPS), :]

    drive0 = drive_at(0)
    drive1 = drive_at(1)
    pair_v[core, 0:16, :] = drive_at(2)
    pair_v[core, 16:32, :] = drive_at(3)
    pair_v[core, 32:40, :] = jnp.broadcast_to(leak_ref[...], (8, 128))
    pair_v[core, 40:48, :] = jnp.broadcast_to(readout_ref[...], (8, 128))
    spikes0 = squash(drive0)
    m1[me] = spikes0

    pl.semaphore_wait(barrier, TP - 1 + pops - 1)


    push(m1.at[me], m1.at[me], plane, m1_send, m1_recv)
    exchanged("m1", m1, TP - 1, m1_send, m1_recv)
    push(rows_src, rows_v.at[me], plane, rows_send, rows_recv, by_core=True)
    exchanged("rows", rows_v, TP - 1, rows_send, rows_recv)

    to_mate = [
        pltpu.make_async_remote_copy(
            src_ref=src,
            dst_ref=dst,
            send_sem=pair_send.at[i],
            recv_sem=pair_recv.at[i],
            device_id=(pop, mate),
            device_id_type=MESH,
        )
        for i, (src, dst) in enumerate(
            (
                (pair_v.at[core], pair_v.at[core]),
                (w_rec_hbm, w_pair.at[core]),
            )
        )
    ]

    def start_mate(i):
        to_mate[i].start()
        arrivals["mate%d" % i] = to_mate[i].wait_recv
        departures.append(to_mate[i].wait_send)

    start_mate(0)
    start_mate(1)

    first = lax.rem(chip, SIDE) * (1 - core) + lax.div(chip, SIDE) * core
    second = lax.div(chip, SIDE) * (1 - core) + lax.rem(chip, SIDE) * core

    def chip_at(u, v):
        return (u * (1 - core) + v * core) + SIDE * (v * (1 - core) + u * core)

    def step(w, by):
        return lax.rem(w + by, SIDE)

    across = [first, step(first, 3), step(first, 1), step(first, 2)]
    v_minus, v_plus, v_far = step(second, 3), step(second, 1), step(second, 2)

    def gather_ops(ref, start, low, total, send_sem, recv_sem):
        def part(slot, half):
            if half == 0:
                return ref.at[slot, pl.ds(start, low)]
            if half == 1:
                return ref.at[slot, pl.ds(start + low, total - low)]
            return ref.at[slot, pl.ds(start, total)]

        def send(slot, to, sem, half=None):
            pltpu.make_async_remote_copy(
                src_ref=part(slot, half),
                dst_ref=part(slot, half),
                send_sem=send_sem,
                recv_sem=recv_sem.at[sem],
                device_id=(pop, 2 * to + core),
                device_id_type=MESH,
            ).start()

        def wait(slot, sem, half=None):
            piece = part(slot, half)
            pltpu.make_async_copy(piece, piece, recv_sem.at[sem]).wait()

        def along(i):
            slot = chip_at(across[i], second)
            send(slot, chip_at(first, v_plus), 4 + 4 * i)
            send(slot, chip_at(first, v_minus), 5 + 4 * i)

        def near(i, onward=True):
            slot = chip_at(across[i], second)
            wait(slot, i - 1)
            send(slot, chip_at(across[3 - i], second), 1 + i, half=i - 1)
            if onward:
                along(i)
            return slot

        def far(onward=True):
            slot = chip_at(across[3], second)
            wait(slot, 2, half=0)
            wait(slot, 3, half=1)
            if onward:
                along(3)
            return slot

        def side_minus(i):
            slot = chip_at(across[i], v_minus)
            wait(slot, 4 + 4 * i)
            send(slot, chip_at(first, v_plus), 6 + 4 * i, half=0)
            return slot

        def side_plus(i):
            slot = chip_at(across[i], v_plus)
            wait(slot, 5 + 4 * i)
            send(slot, chip_at(first, v_minus), 7 + 4 * i, half=1)
            return slot

        def last(i):
            slot = chip_at(across[i], v_far)
            wait(slot, 6 + 4 * i, half=0)
            wait(slot, 7 + 4 * i, half=1)
            return slot

        def begin(onward=True):
            slot = chip_at(first, second)
            send(slot, chip_at(across[2], second), 0)
            send(slot, chip_at(across[1], second), 1)
            if onward:
                along(0)

        return begin, near, far, side_minus, side_plus, last, along

    tt_ref = tt_all.at[core]
    tt_begin, tt_near, tt_far, tt_minus, tt_plus, tt_last, tt_along = gather_ops(
        tt_ref, 0, 64, COLS, tt_send, tt_recv
    )
    tt_begin(onward=False)
    departures.append(bytes_of(tt_ref.at[pl.ds(0, CHIPS - 1)], tt_send))
    departures.append(bytes_of(tt_ref, pair_send.at[2]))
    arrivals["mate2"] = bytes_of(tt_ref, pair_recv.at[2])

    def share(slot):
        pltpu.make_async_remote_copy(
            src_ref=tt_all.at[core, slot],
            dst_ref=tt_all.at[core, slot],
            send_sem=pair_send.at[2],
            recv_sem=pair_recv.at[2],
            device_id=(pop, mate),
            device_id_type=MESH,
        ).start()

    def tt_second():
        for i in range(SIDE):
            tt_along(i)
        for i in range(SIDE):
            share(chip_at(across[i], second))

    def tt_sides():
        for i in range(SIDE):
            share(tt_minus(i))
            share(tt_plus(i))

    def tt_rest():
        for i in range(SIDE):
            share(tt_last(i))

    background += [
        lambda: tt_near(1, onward=False),
        lambda: tt_near(2, onward=False),
        lambda: tt_far(onward=False),
        tt_second,
        tt_sides,
        tt_rest,
    ]

    if pops > 1:
        push(meta.at[pop], meta.at[pop], column, meta_send, meta_recv)
        exchanged("meta", meta, pops - 1, meta_send, meta_recv)

    arrived("w_rec")
    arrived("m1")

    def both(ref, c, low, high):
        return jnp.concatenate([ref[2 * c, low:high, :], ref[2 * c + 1, low:high, :]], axis=1)

    recurrent1 = jnp.zeros((16, COLS), F32)
    for c in range(CHIPS):
        recurrent1 = recurrent1 + dot(
            both(m1, c, 0, 16), w_pair[core, pl.ds(PAIR * c, PAIR), :]
        )
    m2[me] = leak_ref[...] * (drive0 - spikes0.astype(F32)) + (drive1 + recurrent1)

    push(m2.at[me], m2.at[me], plane, m2_send, m2_recv)
    exchanged("m2", m2, TP - 1, m2_send, m2_recv)

    advance(2)
    arrived("rows")
    project1 = jnp.zeros((HALF, EP), F32)
    for c in range(CHIPS):
        project1 = project1 + dot_nt(both(rows_v, c, 0, 16), both(m1, c, 0, 16))
    for e in range(EPIS):
        proj_v[e] = jnp.broadcast_to(sigma_scale * project1[:, e : e + 1], (HALF, 128))

    advance(1)

    arrived("mate0")
    arrived("mate1")
    arrived("m2")

    acc_v[...] = jnp.zeros_like(acc_v)
    accp_v[...] = jnp.zeros_like(accp_v)

    def weights(c):
        rows = pl.ds(pl.multiple_of(PAIR * c, PAIR), PAIR)
        return jnp.concatenate([w_pair[0, rows, :], w_pair[1, rows, :]], axis=1)

    def spread(e):
        return jnp.concatenate([proj_v[e], proj_v[e]], axis=1)

    def step2(i, _):
        for k in range(2):
            c = 2 * i + k
            base = 2.0 * both(m2, c, 0, 16) - 2.0
            post = 2.0 * both(rows_v, c, 16, 32).astype(F32)
            for e in range(EPIS):
                lhs_v[k, HALF * e : HALF * (e + 1), :] = (
                    0.5 + 0.5 * jnp.tanh(base[e : e + 1] + spread(e) * post)
                ).astype(BF16)
        for k in range(2):
            c = 2 * i + k
            acc_v[...] += dot(lhs_v[k], weights(c))
            accp_v[...] += dot_nt(lhs_v[k], both(rows_v, c, 0, 16))
        return 0

    lax.fori_loop(0, CHIPS // 2, step2, 0)

    slot_of = lax.broadcasted_iota(jnp.int32, (KTAB, 128), 0).astype(F32)
    per_group = min(4, pops)

    def group_row(ref, g, row):
        total = ref[per_group * g, row : row + 1, :]
        for k in range(1, per_group):
            total = total + ref[per_group * g + k, row : row + 1, :]
        return total

    def choose_posts():
        if pops > 1:
            arrived("meta")
        for g in range(groups):
            chosen = jnp.where(slot_of == group_row(meta, g, 1), 1.0, 0.0)
            post_all[128 * g : 128 * (g + 1), :] = dot(
                chosen.T.astype(BF16), table_v[...]
            ).astype(BF16)

    leak = jnp.concatenate([pair_v[0, 32:33, :], pair_v[1, 32:33, :]], axis=1)
    readout = jnp.concatenate([pair_v[0, 40:41, :], pair_v[1, 40:41, :]], axis=1)
    drive2 = jnp.concatenate([pair_v[0, 0:16, :], pair_v[1, 0:16, :]], axis=1)
    drive3 = jnp.concatenate([pair_v[0, 16:32, :], pair_v[1, 16:32, :]], axis=1)
    post_here = both(rows_v, chip, 16, 32).astype(F32)
    base_here = both(m2, chip, 0, 16)
    eye = lax.broadcasted_iota(jnp.int32, (HALF, HALF), 0) == lax.broadcasted_iota(
        jnp.int32, (HALF, HALF), 1
    )

    def projection(e):
        square = accp_v[HALF * e : HALF * (e + 1), :]
        own = jnp.sum(jnp.where(eye, square, 0.0), axis=1, keepdims=True)
        return sigma_scale * own * post_here

    first_spikes = both(m1, chip, 0, 16).astype(F32)
    real = lax.broadcasted_iota(jnp.int32, (EP, PAIR), 0) < EPIS
    spike_sum = jnp.broadcast_to(
        jnp.sum(jnp.where(real, first_spikes, 0.0), axis=0, keepdims=True), (HALF, PAIR)
    )
    pieces = [
        gather_ops(spikes_v, PIECE * q, LOW, PIECE, sp_send, sp_recv.at[q]) for q in range(PIECES)
    ]
    departures.append(bytes_of(spikes_v.at[pl.ds(0, CHIPS - 1)], sp_send))
    for e in range(EPIS):
        rows = slice(HALF * e, HALF * (e + 1))
        membrane1 = base_here[e : e + 1] + spread(e) * post_here
        spikes1 = squash(membrane1).astype(F32)
        membrane2 = leak * (membrane1 - spikes1) + (
            drive2[e : e + 1] + acc_v[rows, :] + projection(e)
        )
        spikes2 = squash(membrane2)
        spikes_v[chip, rows, :] = spikes2
        wide = spikes2.astype(F32)
        spike_sum = spike_sum + (spikes1 + wide)
        mem_v[rows, :] = leak * (membrane2 - wide) + drive3[e : e + 1]
        if (e + 1) * HALF % PIECE == 0:
            pieces[e * HALF // PIECE][0]()

    acc_v[...] = jnp.zeros_like(acc_v)
    accp_v[...] = jnp.zeros_like(accp_v)

    def take(c):
        block = spikes_v[c]
        acc_v[...] += dot(block, weights(c))
        accp_v[...] += dot_nt(block, both(rows_v, c, 0, 16))

    take(chip)
    order = [(1, 1), (1, 2), (3, 0), (4, 0), (2, None), (3, 1), (4, 1), (3, 2), (4, 2), (5, 0), (3, 3)]
    order += [(4, 3), (5, 1), (5, 2), (5, 3)]
    stage = [0] * 4 + [1] * 5 + [2] * 3 + [3] * 3
    events = sorted((stage[i], q, i) for q in range(PIECES) for i in range(len(order)))
    for when, (_, q, i) in enumerate(events):
        kind, which = order[i]
        slot = pieces[q][kind]() if which is None else pieces[q][kind](which)
        if q == PIECES - 1:
            take(slot)
        if when == len(events) // 2:
            choose_posts()

    for e in range(EPIS):
        rows = slice(HALF * e, HALF * (e + 1))
        membrane3 = mem_v[rows, :] + (acc_v[rows, :] + projection(e))
        spike_sum = spike_sum + squash(membrane3).astype(F32)

    reward = jnp.sum(spike_sum * readout, axis=1, keepdims=True)
    lane16 = lax.broadcasted_iota(jnp.int32, (HALF, 128), 1)
    member16 = lax.broadcasted_iota(jnp.int32, (HALF, 128), 0)
    mine = lane16 == member16 + (lax.rem(pop, 4) * 32 + core * HALF)
    m3[me] = jnp.sum(jnp.where(mine, reward, 0.0), axis=0, keepdims=True)

    push(m3.at[me], m3.at[me], plane, m3_send, m3_recv)
    exchanged("m3", m3, TP - 1, m3_send, m3_recv)

    advance(1)

    arrived("m3")
    returns_row = jnp.sum(m3[...], axis=0) / (EPIS * STEPS)
    returns_ref[...] = (
        returns_row[:, 0:32] + returns_row[:, 32:64] + returns_row[:, 64:96] + returns_row[:, 96:128]
    )
    ranks = rank_ref[...].astype(F32) / (32 * pops - 1) - 0.5
    m4[pop] = placed(ranks) + returns_row

    if pops > 1:
        push(m4.at[pop], m4.at[pop], column, m4_send, m4_recv)
        exchanged("m4", m4, pops - 1, m4_send, m4_recv)
    advance(2)
    saves = [
        pltpu.make_async_copy(tt_all.at[part], tt_hbm.at[part], local_sem.at[15 + i])
        for i, part in enumerate((core, 1 - core))
    ]
    saves.append(pltpu.make_async_copy(returns_ref, returns_hbm, local_sem.at[17]))
    saves[0].start()
    saves[2].start()
    arrived("mate2")
    saves[1].start()
    if pops > 1:
        arrived("m4")

    high, low = [], []
    for g in range(groups):
        scaled = jnp.where(slot_of == group_row(meta, g, 0), group_row(m4, g, 0), 0.0)
        top = scaled.astype(BF16)
        high.append(top)
        low.append((scaled - top.astype(F32)).astype(BF16))
    mixed = dot(jnp.concatenate(high, axis=1), post_all[...]) + dot(
        jnp.concatenate(low, axis=1), post_all[...]
    )
    mixed = mixed * jnp.sqrt(jnp.float32(12.0 / (32 * pops)))
    top = mixed.astype(BF16)
    split_ref[...] = jnp.concatenate([top, (mixed - top.astype(F32)).astype(BF16)], axis=1)
    saves.append(pltpu.make_async_copy(split_ref, split_hbm, local_sem.at[18]))
    saves[3].start()
    finish()
    for save in saves:
        save.wait()


def gradient(
    returns_in, tt_hbm, split_hbm, returns_hbm, grad_hbm, tt_v, split_v, grad_v, in_sems, out_sems
):
    blocks = CHIPS // 4
    split_load = pltpu.make_async_copy(split_hbm, split_v, in_sems.at[blocks])
    split_load.start()
    loads = [
        pltpu.make_async_copy(
            tt_hbm.at[:, pl.ds(4 * q, 4)], tt_v.at[:, pl.ds(4 * q, 4)], in_sems.at[q]
        )
        for q in range(blocks)
    ]
    for load in loads:
        load.start()
    returns_copy = pltpu.make_async_copy(returns_in, returns_hbm, out_sems.at[blocks])
    returns_copy.start()
    split_load.wait()
    split = split_v[...]
    stores = []
    for q in range(blocks):
        loads[q].wait()
        for k in range(2):
            block = tt_v[k, 4 * q : 4 * q + 4].reshape(4 * COLS, KTAB)
            both_parts = dot(block, split)
            rows = (both_parts[:, 0:COLS] + both_parts[:, COLS:PAIR]).astype(BF16)
            for n in range(4):
                start = PAIR * (4 * q + n) + COLS * k
                grad_v[start : start + COLS, :] = rows[COLS * n : COLS * (n + 1)]
        part = pl.ds(4 * PAIR * q, 4 * PAIR)
        stores.append(pltpu.make_async_copy(grad_v.at[part], grad_hbm.at[part], out_sems.at[q]))
        stores[-1].start()
    for store in stores + [returns_copy]:
        store.wait()


def shards(
    in_spikes, w_in, w_rec, leak_rate, neuron_bias, readout, pert_table, pert_idx, member_ranks
):
    pops = lax.axis_size("pop")
    hbm = pl.BlockSpec(memory_space=pltpu.HBM)
    dma = pltpu.SemaphoreType.DMA
    returns, table_t, split = pl.pallas_call(
        functools.partial(kernel, pops),
        out_shape=(
            jax.ShapeDtypeStruct((1, 32), F32),
            jax.ShapeDtypeStruct((2, CHIPS, COLS, KTAB), BF16),
            jax.ShapeDtypeStruct((KTAB, PAIR), BF16),
        ),
        in_specs=[hbm] * 9,
        out_specs=(hbm, hbm, hbm),
        scratch_shapes=[
            pltpu.VMEM((1, 32), F32),
            pltpu.VMEM((KTAB, PAIR), BF16),
            pltpu.VMEM((1, COLS), F32),
            pltpu.VMEM((1, COLS), F32),
            pltpu.VMEM((1, COLS), F32),
            pltpu.VMEM((2, 32), jnp.int32),
            pltpu.VMEM((1, 32), jnp.int32),
            pltpu.VMEM((2, CHIPS, COLS, KTAB), BF16),
            pltpu.VMEM((EPIS, STEPS, NEUR), jnp.int32),
            pltpu.VMEM((NEUR, COLS), BF16),
            pltpu.VMEM((2, NEUR, COLS), BF16),
            pltpu.VMEM((STEPS * EP, NEUR), F32),
            pltpu.VMEM((STEPS * EP, COLS), F32),
            pltpu.VMEM((KTAB, COLS), BF16),
            pltpu.VMEM((2, 32, COLS), BF16),
            pltpu.VMEM((TP, 32, COLS), BF16),
            pltpu.VMEM((TP, EP, COLS), BF16),
            pltpu.VMEM((TP, EP, COLS), F32),
            pltpu.VMEM((2, 48, COLS), F32),
            pltpu.VMEM((pops, 8, 128), F32),
            pltpu.VMEM((TP, 1, 128), F32),
            pltpu.VMEM((pops, 1, 128), F32),
            pltpu.VMEM((EPIS, HALF, 128), F32),
            pltpu.VMEM((2, ROWS, PAIR), BF16),
            pltpu.VMEM((ROWS, PAIR), F32),
            pltpu.VMEM((ROWS, HALF), F32),
            pltpu.VMEM((ROWS, PAIR), F32),
            pltpu.VMEM((CHIPS, ROWS, PAIR), BF16),
            pltpu.VMEM((128 * max(1, pops // 4), COLS), BF16),
            dma((19,)),
            dma,
            dma,
            dma,
            dma,
            dma,
            dma,
            dma,
            dma,
            dma,
            dma,
            dma,
            dma,
            dma((3,)),
            dma((3,)),
            dma,
            dma((20,)),
            dma,
            dma((PIECES, 20)),
        ],
        compiler_params=pltpu.CompilerParams(
            collective_id=0, has_side_effects=True, vmem_limit_bytes=60 * 1024 * 1024
        ),
        name="rollout",
    )(
        in_spikes.transpose(1, 0, 2),
        w_in,
        w_rec,
        leak_rate.reshape(1, COLS),
        neuron_bias.reshape(1, COLS),
        readout.reshape(1, COLS),
        pert_table,
        pert_idx.T,
        member_ranks.reshape(1, 32),
    )
    returns, grad_rec = pl.pallas_call(
        gradient,
        out_shape=(
            jax.ShapeDtypeStruct((1, 32), F32),
            jax.ShapeDtypeStruct((NEUR, COLS), BF16),
        ),
        in_specs=[hbm, hbm, hbm],
        out_specs=(hbm, hbm),
        scratch_shapes=[
            pltpu.VMEM((2, CHIPS, COLS, KTAB), BF16),
            pltpu.VMEM((KTAB, PAIR), BF16),
            pltpu.VMEM((NEUR, COLS), BF16),
            dma((CHIPS // 4 + 1,)),
            dma((CHIPS // 4 + 1,)),
        ],
        compiler_params=pltpu.CompilerParams(vmem_limit_bytes=60 * 1024 * 1024),
        name="gradient",
    )(returns, table_t, split)
    return returns.reshape(32), grad_rec


def solution(mesh):
    placed = (
        P(),
        P(None, "tp"),
        P(None, "tp"),
        P("tp"),
        P("tp"),
        P("tp"),
        P(None, "tp"),
        P("pop", None),
        P("pop"),
    )
    return jax.shard_map(
        shards, mesh=mesh, in_specs=placed, out_specs=(P("pop"), P(None, "tp")), check_vma=False
    )
```

```python
import functools

import jax
import jax.numpy as jnp
from jax import lax
from jax.experimental import pallas as pl
from jax.experimental.pallas import tpu as pltpu
from jax.sharding import PartitionSpec as P

MESH = pl.DeviceIdType.MESH
F32 = jnp.float32
BF16 = jnp.bfloat16
sigma_scale = 0.01

STEPS = 4
EPIS = 15
EP = 16
SIDE = 4
CHIPS = 16
TP = 32
COLS = 128
PAIR = 256
HALF = 16
ROWS = EPIS * HALF
PIECES = 3
PIECE = ROWS // PIECES
LOW = 48
NEUR = 4096
KTAB = 256
BLOCK = 2

NT = (((1,), (1,)), ((), ()))
TN = (((0,), (0,)), ((), ()))


def dot(left, right):
    return jnp.dot(left, right, preferred_element_type=F32)


def dot_nt(left, right):
    return lax.dot_general(left, right, NT, preferred_element_type=F32)


def squash(membrane):
    return (0.5 + 0.5 * jnp.tanh(2.0 * membrane - 2.0)).astype(BF16)


def kernel(
    pops,
    in_hbm,
    w_in_hbm,
    w_rec_hbm,
    leak_hbm,
    bias_hbm,
    readout_hbm,
    table_hbm,
    idx_hbm,
    rank_hbm,
    returns_hbm,
    tt_hbm,
    split_hbm,
    returns_ref,
    split_ref,
    leak_ref,
    bias_ref,
    readout_ref,
    idx_ref,
    rank_ref,
    tt_all,
    spk_v,
    w_in_v,
    w_pair,
    x_v,
    drive_v,
    table_v,
    rows_src,
    rows_v,
    m1,
    m2,
    pair_v,
    meta,
    m3,
    m4,
    proj_v,
    lhs_v,
    acc_v,
    accp_v,
    mem_v,
    spikes_v,
    post_all,
    local_sem,
    m1_send,
    m1_recv,
    rows_send,
    rows_recv,
    m2_send,
    m2_recv,
    m3_send,
    m3_recv,
    m4_send,
    m4_recv,
    meta_send,
    meta_recv,
    pair_send,
    pair_recv,
    tt_send,
    tt_recv,
    sp_send,
    sp_recv,
):
    pop = lax.axis_index("pop")
    me = lax.axis_index("tp")
    core = lax.rem(me, 2)
    chip = lax.div(me, 2)
    mate = me + 1 - 2 * core
    groups = max(1, pops // 4)
    quarter = NEUR // 4
    parts = [pl.ds(quarter * q, quarter) for q in range(4)]
    loads = [pltpu.make_async_copy(table_hbm, table_v, local_sem.at[0])]
    for q, part in enumerate(parts):
        loads += [
            pltpu.make_async_copy(
                in_hbm.at[:, :, part], spk_v.at[:, :, part], local_sem.at[2 * q + 1]
            ),
            pltpu.make_async_copy(w_in_hbm.at[part], w_in_v.at[part], local_sem.at[2 * q + 2]),
        ]
    loads.append(pltpu.make_async_copy(w_rec_hbm, w_pair.at[core], local_sem.at[9]))
    small = [
        pltpu.make_async_copy(src, dst, local_sem.at[10 + i])
        for i, (src, dst) in enumerate(
            (
                (idx_hbm, idx_ref),
                (leak_hbm, leak_ref),
                (bias_hbm, bias_ref),
                (readout_hbm, readout_ref),
                (rank_hbm, rank_ref),
            )
        )
    ]
    small[0].start()
    for load in loads + small[1:]:
        load.start()

    arrivals, departures, background = {"w_rec": loads[9].wait}, [], []

    def bytes_of(ref, sem):
        return pltpu.make_async_copy(ref, ref, sem).wait

    def arrived(name):
        arrivals.pop(name)()

    def advance(count):
        for _ in range(count):
            background.pop(0)()

    def finish():
        advance(len(background))
        for name in list(arrivals):
            arrived(name)
        for departed in departures:
            departed()

    def exchanged(name, ref, peers, send_sem, recv_sem):
        part = ref.at[pl.ds(0, peers)]
        arrivals[name] = bytes_of(part, recv_sem)
        departures.append(bytes_of(part, send_sem))

    x, y = lax.rem(chip, SIDE), lax.div(chip, SIDE)

    def hops(shift, size):
        return min(shift, size - shift)

    shifts = sorted(
        ((dx, dy, dc) for dx in range(SIDE) for dy in range(SIDE) for dc in range(2)),
        key=lambda s: -(hops(s[0], SIDE) + hops(s[1], SIDE)),
    )
    plane = [
        (pop, 2 * (SIDE * lax.rem(y + dy, SIDE) + lax.rem(x + dx, SIDE)) + (1 - core if dc else core))
        for dx, dy, dc in shifts
        if dx + dy + dc > 0
    ]
    same_core = [dc == 0 for dx, dy, dc in shifts if dx + dy + dc > 0]
    column = [
        (lax.rem(pop + k, pops), me) for k in sorted(range(1, pops), key=lambda k: -hops(k, pops))
    ]

    barrier = pltpu.get_barrier_semaphore()
    for peer in column + plane:
        pl.semaphore_signal(barrier, inc=1, device_id=peer, device_id_type=MESH)

    def push(source, target, peers, send_sem, recv_sem, by_core=False):
        for n, peer in enumerate(peers):
            src = source
            if by_core:
                src = source.at[core if same_core[n] else 1 - core]
            pltpu.make_async_remote_copy(
                src_ref=src,
                dst_ref=target,
                send_sem=send_sem,
                recv_sem=recv_sem,
                device_id=peer,
                device_id_type=MESH,
            ).start()

    for load in small[1:]:
        load.wait()
    drive = jnp.broadcast_to(bias_ref[...], (STEPS * EP, COLS))
    x_v[STEPS * EPIS :, :] = jnp.zeros((STEPS, NEUR), F32)
    for q, part in enumerate(parts):
        loads[2 * q + 1].wait()
        for e in range(EPIS):
            x_v[STEPS * e : STEPS * (e + 1), part] = spk_v[e, :, part].astype(F32)
        loads[2 * q + 2].wait()
        drive = drive + dot(x_v[:, part].astype(BF16), w_in_v[part, :])
    drive_v[...] = drive

    def drive_at(t):
        return drive_v[pl.ds(t, EP, stride=STEPS), :]

    drive0 = drive_at(0)
    drive1 = drive_at(1)
    spikes0 = squash(drive0)
    m1[me] = spikes0

    pl.semaphore_wait(barrier, TP - 1 + pops - 1)


    push(m1.at[me], m1.at[me], plane, m1_send, m1_recv)
    exchanged("m1", m1, TP - 1, m1_send, m1_recv)

    lane1 = lax.broadcasted_iota(jnp.int32, (1, 128), 1)
    here = lax.div(lane1, 32) == lax.rem(pop, 4)

    def placed(row):
        return jnp.where(here, jnp.concatenate([row, row, row, row], axis=1), 0.0)

    small[0].wait()
    indices = idx_ref[...].astype(F32)
    meta[pop, 0:1, :] = placed(indices[0:1])
    meta[pop, 1:2, :] = placed(indices[1:2])
    meta[pop, 2:8, :] = jnp.zeros((6, 128), F32)

    loads[0].wait()
    spot = lax.broadcasted_iota(jnp.int32, (32, KTAB), 1).astype(F32)
    diagonal = lax.broadcasted_iota(jnp.int32, (32, 32), 0) == lax.broadcasted_iota(
        jnp.int32, (32, 32), 1
    )

    def picks(row):
        column = jnp.sum(jnp.where(diagonal, row, 0.0), axis=1, keepdims=True)
        return jnp.where(spot == column, 1.0, 0.0).astype(BF16)

    pick = jnp.concatenate([picks(indices[0:1]), picks(indices[1:2])], axis=0)
    picked = dot(pick, table_v[...]).astype(BF16)
    for half in range(2):
        rows_src[half, 0:16, :] = picked[16 * half : 16 * half + 16]
        rows_src[half, 16:32, :] = picked[32 + 16 * half : 48 + 16 * half]
    rows_v[me] = rows_src[core]
    tt_all[core, chip] = table_v[...].astype(F32).T.astype(BF16)

    pair_v[core, 0:16, :] = drive_at(2)
    pair_v[core, 16:32, :] = drive_at(3)
    pair_v[core, 32:40, :] = jnp.broadcast_to(leak_ref[...], (8, 128))
    pair_v[core, 40:48, :] = jnp.broadcast_to(readout_ref[...], (8, 128))
    push(rows_src, rows_v.at[me], plane, rows_send, rows_recv, by_core=True)
    exchanged("rows", rows_v, TP - 1, rows_send, rows_recv)

    to_mate = [
        pltpu.make_async_remote_copy(
            src_ref=src,
            dst_ref=dst,
            send_sem=pair_send.at[i],
            recv_sem=pair_recv.at[i],
            device_id=(pop, mate),
            device_id_type=MESH,
        )
        for i, (src, dst) in enumerate(
            (
                (pair_v.at[core], pair_v.at[core]),
                (w_rec_hbm, w_pair.at[core]),
            )
        )
    ]

    def start_mate(i):
        to_mate[i].start()
        arrivals["mate%d" % i] = to_mate[i].wait_recv
        departures.append(to_mate[i].wait_send)

    start_mate(0)
    start_mate(1)

    first = lax.rem(chip, SIDE) * (1 - core) + lax.div(chip, SIDE) * core
    second = lax.div(chip, SIDE) * (1 - core) + lax.rem(chip, SIDE) * core

    def chip_at(u, v):
        return (u * (1 - core) + v * core) + SIDE * (v * (1 - core) + u * core)

    def step(w, by):
        return lax.rem(w + by, SIDE)

    across = [first, step(first, 3), step(first, 1), step(first, 2)]
    v_minus, v_plus, v_far = step(second, 3), step(second, 1), step(second, 2)

    def gather_ops(ref, start, low, total, send_sem, recv_sem):
        def part(slot, half):
            if half == 0:
                return ref.at[slot, pl.ds(start, low)]
            if half == 1:
                return ref.at[slot, pl.ds(start + low, total - low)]
            return ref.at[slot, pl.ds(start, total)]

        def send(slot, to, sem, half=None):
            pltpu.make_async_remote_copy(
                src_ref=part(slot, half),
                dst_ref=part(slot, half),
                send_sem=send_sem,
                recv_sem=recv_sem.at[sem],
                device_id=(pop, 2 * to + core),
                device_id_type=MESH,
            ).start()

        def wait(slot, sem, half=None):
            piece = part(slot, half)
            pltpu.make_async_copy(piece, piece, recv_sem.at[sem]).wait()

        def along(i):
            slot = chip_at(across[i], second)
            send(slot, chip_at(first, v_plus), 4 + 4 * i)
            send(slot, chip_at(first, v_minus), 5 + 4 * i)

        def near(i, onward=True):
            slot = chip_at(across[i], second)
            wait(slot, i - 1)
            send(slot, chip_at(across[3 - i], second), 1 + i, half=i - 1)
            if onward:
                along(i)
            return slot

        def far(onward=True):
            slot = chip_at(across[3], second)
            wait(slot, 2, half=0)
            wait(slot, 3, half=1)
            if onward:
                along(3)
            return slot

        def side_minus(i):
            slot = chip_at(across[i], v_minus)
            wait(slot, 4 + 4 * i)
            send(slot, chip_at(first, v_plus), 6 + 4 * i, half=0)
            return slot

        def side_plus(i):
            slot = chip_at(across[i], v_plus)
            wait(slot, 5 + 4 * i)
            send(slot, chip_at(first, v_minus), 7 + 4 * i, half=1)
            return slot

        def last(i):
            slot = chip_at(across[i], v_far)
            wait(slot, 6 + 4 * i, half=0)
            wait(slot, 7 + 4 * i, half=1)
            return slot

        def begin(onward=True):
            slot = chip_at(first, second)
            send(slot, chip_at(across[2], second), 0)
            send(slot, chip_at(across[1], second), 1)
            if onward:
                along(0)

        return begin, near, far, side_minus, side_plus, last, along

    tt_ref = tt_all.at[core]
    tt_begin, tt_near, tt_far, tt_minus, tt_plus, tt_last, tt_along = gather_ops(
        tt_ref, 0, 64, COLS, tt_send, tt_recv
    )
    tt_begin(onward=False)
    departures.append(bytes_of(tt_ref.at[pl.ds(0, CHIPS - 1)], tt_send))
    departures.append(bytes_of(tt_ref, pair_send.at[2]))
    arrivals["mate2"] = bytes_of(tt_ref, pair_recv.at[2])

    def share(slot):
        pltpu.make_async_remote_copy(
            src_ref=tt_all.at[core, slot],
            dst_ref=tt_all.at[core, slot],
            send_sem=pair_send.at[2],
            recv_sem=pair_recv.at[2],
            device_id=(pop, mate),
            device_id_type=MESH,
        ).start()

    def tt_second():
        for i in range(SIDE):
            tt_along(i)
        for i in range(SIDE):
            share(chip_at(across[i], second))

    def tt_sides():
        for i in range(SIDE):
            share(tt_minus(i))
            share(tt_plus(i))

    def tt_rest():
        for i in range(SIDE):
            share(tt_last(i))

    background += [
        lambda: tt_near(1, onward=False),
        lambda: tt_near(2, onward=False),
        lambda: tt_far(onward=False),
        tt_second,
        tt_sides,
        tt_rest,
    ]

    if pops > 1:
        push(meta.at[pop], meta.at[pop], column, meta_send, meta_recv)
        exchanged("meta", meta, pops - 1, meta_send, meta_recv)

    arrived("w_rec")
    arrived("m1")

    def both(ref, c, low, high):
        return jnp.concatenate([ref[2 * c, low:high, :], ref[2 * c + 1, low:high, :]], axis=1)

    recurrent1 = jnp.zeros((16, COLS), F32)
    for c in range(CHIPS):
        recurrent1 = recurrent1 + dot(
            both(m1, c, 0, 16), w_pair[core, pl.ds(PAIR * c, PAIR), :]
        )
    m2[me] = leak_ref[...] * (drive0 - spikes0.astype(F32)) + (drive1 + recurrent1)

    push(m2.at[me], m2.at[me], plane, m2_send, m2_recv)
    exchanged("m2", m2, TP - 1, m2_send, m2_recv)

    advance(2)
    arrived("rows")
    project1 = jnp.zeros((HALF, EP), F32)
    for c in range(CHIPS):
        project1 = project1 + dot_nt(both(rows_v, c, 0, 16), both(m1, c, 0, 16))
    for e in range(EPIS):
        proj_v[e] = jnp.broadcast_to(sigma_scale * project1[:, e : e + 1], (HALF, 128))

    advance(1)

    arrived("mate0")
    arrived("mate1")
    arrived("m2")

    acc_v[...] = jnp.zeros_like(acc_v)
    accp_v[...] = jnp.zeros_like(accp_v)

    def weights(c):
        rows = pl.ds(pl.multiple_of(PAIR * c, PAIR), PAIR)
        return jnp.concatenate([w_pair[0, rows, :], w_pair[1, rows, :]], axis=1)

    def spread(e):
        return jnp.concatenate([proj_v[e], proj_v[e]], axis=1)

    def step2(i, _):
        for k in range(2):
            c = 2 * i + k
            base = 2.0 * both(m2, c, 0, 16) - 2.0
            post = 2.0 * both(rows_v, c, 16, 32).astype(F32)
            for e in range(EPIS):
                lhs_v[k, HALF * e : HALF * (e + 1), :] = (
                    0.5 + 0.5 * jnp.tanh(base[e : e + 1] + spread(e) * post)
                ).astype(BF16)
        for k in range(2):
            c = 2 * i + k
            acc_v[...] += dot(lhs_v[k], weights(c))
            accp_v[...] += dot_nt(lhs_v[k], both(rows_v, c, 0, 16))
        return 0

    lax.fori_loop(0, CHIPS // 2, step2, 0)

    slot_of = lax.broadcasted_iota(jnp.int32, (KTAB, 128), 0).astype(F32)
    per_group = min(4, pops)

    def group_row(ref, g, row):
        total = ref[per_group * g, row : row + 1, :]
        for k in range(1, per_group):
            total = total + ref[per_group * g + k, row : row + 1, :]
        return total

    def choose_posts():
        if pops > 1:
            arrived("meta")
        for g in range(groups):
            chosen = jnp.where(slot_of == group_row(meta, g, 1), 1.0, 0.0)
            post_all[128 * g : 128 * (g + 1), :] = dot(
                chosen.T.astype(BF16), table_v[...]
            ).astype(BF16)

    leak = jnp.concatenate([pair_v[0, 32:33, :], pair_v[1, 32:33, :]], axis=1)
    readout = jnp.concatenate([pair_v[0, 40:41, :], pair_v[1, 40:41, :]], axis=1)
    drive2 = jnp.concatenate([pair_v[0, 0:16, :], pair_v[1, 0:16, :]], axis=1)
    drive3 = jnp.concatenate([pair_v[0, 16:32, :], pair_v[1, 16:32, :]], axis=1)
    post_here = both(rows_v, chip, 16, 32).astype(F32)
    base_here = both(m2, chip, 0, 16)
    eye = lax.broadcasted_iota(jnp.int32, (HALF, HALF), 0) == lax.broadcasted_iota(
        jnp.int32, (HALF, HALF), 1
    )

    def projection(e):
        square = accp_v[HALF * e : HALF * (e + 1), :]
        own = jnp.sum(jnp.where(eye, square, 0.0), axis=1, keepdims=True)
        return sigma_scale * own * post_here

    first_spikes = both(m1, chip, 0, 16).astype(F32)
    real = lax.broadcasted_iota(jnp.int32, (EP, PAIR), 0) < EPIS
    spike_sum = jnp.broadcast_to(
        jnp.sum(jnp.where(real, first_spikes, 0.0), axis=0, keepdims=True), (HALF, PAIR)
    )
    pieces = [
        gather_ops(spikes_v, PIECE * q, LOW, PIECE, sp_send, sp_recv.at[q]) for q in range(PIECES)
    ]
    departures.append(bytes_of(spikes_v.at[pl.ds(0, CHIPS - 1)], sp_send))
    for e in range(EPIS):
        rows = slice(HALF * e, HALF * (e + 1))
        membrane1 = base_here[e : e + 1] + spread(e) * post_here
        spikes1 = squash(membrane1).astype(F32)
        membrane2 = leak * (membrane1 - spikes1) + (
            drive2[e : e + 1] + acc_v[rows, :] + projection(e)
        )
        spikes2 = squash(membrane2)
        spikes_v[chip, rows, :] = spikes2
        wide = spikes2.astype(F32)
        spike_sum = spike_sum + (spikes1 + wide)
        mem_v[rows, :] = leak * (membrane2 - wide) + drive3[e : e + 1]
        if (e + 1) * HALF % PIECE == 0:
            pieces[e * HALF // PIECE][0]()

    acc_v[...] = jnp.zeros_like(acc_v)
    accp_v[...] = jnp.zeros_like(accp_v)

    def take(c):
        block = spikes_v[c]
        acc_v[...] += dot(block, weights(c))
        accp_v[...] += dot_nt(block, both(rows_v, c, 0, 16))

    take(chip)
    order = [(1, 1), (1, 2), (3, 0), (4, 0), (2, None), (3, 1), (4, 1), (3, 2), (4, 2), (5, 0), (3, 3)]
    order += [(4, 3), (5, 1), (5, 2), (5, 3)]
    stage = [0] * 4 + [1] * 5 + [2] * 3 + [3] * 3
    events = sorted((stage[i], q, i) for q in range(PIECES) for i in range(len(order)))
    for when, (_, q, i) in enumerate(events):
        kind, which = order[i]
        slot = pieces[q][kind]() if which is None else pieces[q][kind](which)
        if q == PIECES - 1:
            take(slot)
        if when == len(events) // 2:
            choose_posts()

    for e in range(EPIS):
        rows = slice(HALF * e, HALF * (e + 1))
        membrane3 = mem_v[rows, :] + (acc_v[rows, :] + projection(e))
        spike_sum = spike_sum + squash(membrane3).astype(F32)

    reward = jnp.sum(spike_sum * readout, axis=1, keepdims=True)
    lane16 = lax.broadcasted_iota(jnp.int32, (HALF, 128), 1)
    member16 = lax.broadcasted_iota(jnp.int32, (HALF, 128), 0)
    mine = lane16 == member16 + (lax.rem(pop, 4) * 32 + core * HALF)
    m3[me] = jnp.sum(jnp.where(mine, reward, 0.0), axis=0, keepdims=True)

    push(m3.at[me], m3.at[me], plane, m3_send, m3_recv)
    exchanged("m3", m3, TP - 1, m3_send, m3_recv)

    advance(1)

    arrived("m3")
    returns_row = jnp.sum(m3[...], axis=0) / (EPIS * STEPS)
    returns_ref[...] = (
        returns_row[:, 0:32] + returns_row[:, 32:64] + returns_row[:, 64:96] + returns_row[:, 96:128]
    )
    ranks = rank_ref[...].astype(F32) / (32 * pops - 1) - 0.5
    m4[pop] = placed(ranks) + returns_row

    if pops > 1:
        push(m4.at[pop], m4.at[pop], column, m4_send, m4_recv)
        exchanged("m4", m4, pops - 1, m4_send, m4_recv)
    advance(2)
    saves = [
        pltpu.make_async_copy(tt_all.at[part], tt_hbm.at[part], local_sem.at[15 + i])
        for i, part in enumerate((core, 1 - core))
    ]
    saves.append(pltpu.make_async_copy(returns_ref, returns_hbm, local_sem.at[17]))
    saves[0].start()
    saves[2].start()
    arrived("mate2")
    saves[1].start()
    if pops > 1:
        arrived("m4")

    high, low = [], []
    for g in range(groups):
        scaled = jnp.where(slot_of == group_row(meta, g, 0), group_row(m4, g, 0), 0.0)
        top = scaled.astype(BF16)
        high.append(top)
        low.append((scaled - top.astype(F32)).astype(BF16))
    mixed = dot(jnp.concatenate(high, axis=1), post_all[...]) + dot(
        jnp.concatenate(low, axis=1), post_all[...]
    )
    mixed = mixed * jnp.sqrt(jnp.float32(12.0 / (32 * pops)))
    top = mixed.astype(BF16)
    split_ref[...] = jnp.concatenate([top, (mixed - top.astype(F32)).astype(BF16)], axis=1)
    saves.append(pltpu.make_async_copy(split_ref, split_hbm, local_sem.at[18]))
    saves[3].start()
    finish()
    for save in saves:
        save.wait()


def gradient(
    returns_in, tt_hbm, split_hbm, returns_hbm, grad_hbm, tt_v, split_v, grad_v, in_sems, out_sems
):
    blocks = CHIPS // BLOCK
    split_load = pltpu.make_async_copy(split_hbm, split_v, in_sems.at[blocks])
    split_load.start()
    loads = [
        pltpu.make_async_copy(
            tt_hbm.at[:, pl.ds(BLOCK * q, BLOCK)], tt_v.at[:, pl.ds(BLOCK * q, BLOCK)], in_sems.at[q]
        )
        for q in range(blocks)
    ]
    for load in loads:
        load.start()
    returns_copy = pltpu.make_async_copy(returns_in, returns_hbm, out_sems.at[blocks])
    returns_copy.start()
    split_load.wait()
    split = split_v[...]
    stores = []
    for q in range(blocks):
        loads[q].wait()
        for k in range(2):
            block = tt_v[k, BLOCK * q : BLOCK * (q + 1)].reshape(BLOCK * COLS, KTAB)
            both_parts = dot(block, split)
            rows = (both_parts[:, 0:COLS] + both_parts[:, COLS:PAIR]).astype(BF16)
            for n in range(BLOCK):
                start = PAIR * (BLOCK * q + n) + COLS * k
                grad_v[start : start + COLS, :] = rows[COLS * n : COLS * (n + 1)]
        part = pl.ds(BLOCK * PAIR * q, BLOCK * PAIR)
        stores.append(pltpu.make_async_copy(grad_v.at[part], grad_hbm.at[part], out_sems.at[q]))
        stores[-1].start()
    for store in stores + [returns_copy]:
        store.wait()


def shards(
    in_spikes, w_in, w_rec, leak_rate, neuron_bias, readout, pert_table, pert_idx, member_ranks
):
    pops = lax.axis_size("pop")
    hbm = pl.BlockSpec(memory_space=pltpu.HBM)
    dma = pltpu.SemaphoreType.DMA
    returns, table_t, split = pl.pallas_call(
        functools.partial(kernel, pops),
        out_shape=(
            jax.ShapeDtypeStruct((1, 32), F32),
            jax.ShapeDtypeStruct((2, CHIPS, COLS, KTAB), BF16),
            jax.ShapeDtypeStruct((KTAB, PAIR), BF16),
        ),
        in_specs=[hbm] * 9,
        out_specs=(hbm, hbm, hbm),
        scratch_shapes=[
            pltpu.VMEM((1, 32), F32),
            pltpu.VMEM((KTAB, PAIR), BF16),
            pltpu.VMEM((1, COLS), F32),
            pltpu.VMEM((1, COLS), F32),
            pltpu.VMEM((1, COLS), F32),
            pltpu.VMEM((2, 32), jnp.int32),
            pltpu.VMEM((1, 32), jnp.int32),
            pltpu.VMEM((2, CHIPS, COLS, KTAB), BF16),
            pltpu.VMEM((EPIS, STEPS, NEUR), jnp.int32),
            pltpu.VMEM((NEUR, COLS), BF16),
            pltpu.VMEM((2, NEUR, COLS), BF16),
            pltpu.VMEM((STEPS * EP, NEUR), F32),
            pltpu.VMEM((STEPS * EP, COLS), F32),
            pltpu.VMEM((KTAB, COLS), BF16),
            pltpu.VMEM((2, 32, COLS), BF16),
            pltpu.VMEM((TP, 32, COLS), BF16),
            pltpu.VMEM((TP, EP, COLS), BF16),
            pltpu.VMEM((TP, EP, COLS), F32),
            pltpu.VMEM((2, 48, COLS), F32),
            pltpu.VMEM((pops, 8, 128), F32),
            pltpu.VMEM((TP, 1, 128), F32),
            pltpu.VMEM((pops, 1, 128), F32),
            pltpu.VMEM((EPIS, HALF, 128), F32),
            pltpu.VMEM((2, ROWS, PAIR), BF16),
            pltpu.VMEM((ROWS, PAIR), F32),
            pltpu.VMEM((ROWS, HALF), F32),
            pltpu.VMEM((ROWS, PAIR), F32),
            pltpu.VMEM((CHIPS, ROWS, PAIR), BF16),
            pltpu.VMEM((128 * max(1, pops // 4), COLS), BF16),
            dma((19,)),
            dma,
            dma,
            dma,
            dma,
            dma,
            dma,
            dma,
            dma,
            dma,
            dma,
            dma,
            dma,
            dma((3,)),
            dma((3,)),
            dma,
            dma((20,)),
            dma,
            dma((PIECES, 20)),
        ],
        compiler_params=pltpu.CompilerParams(
            collective_id=0, has_side_effects=True, vmem_limit_bytes=60 * 1024 * 1024
        ),
        name="rollout",
    )(
        in_spikes.transpose(1, 0, 2),
        w_in,
        w_rec,
        leak_rate.reshape(1, COLS),
        neuron_bias.reshape(1, COLS),
        readout.reshape(1, COLS),
        pert_table,
        pert_idx.T,
        member_ranks.reshape(1, 32),
    )
    returns, grad_rec = pl.pallas_call(
        gradient,
        out_shape=(
            jax.ShapeDtypeStruct((1, 32), F32),
            jax.ShapeDtypeStruct((NEUR, COLS), BF16),
        ),
        in_specs=[hbm, hbm, hbm],
        out_specs=(hbm, hbm),
        scratch_shapes=[
            pltpu.VMEM((2, CHIPS, COLS, KTAB), BF16),
            pltpu.VMEM((KTAB, PAIR), BF16),
            pltpu.VMEM((NEUR, COLS), BF16),
            dma((CHIPS // BLOCK + 1,)),
            dma((CHIPS // BLOCK + 1,)),
        ],
        compiler_params=pltpu.CompilerParams(vmem_limit_bytes=60 * 1024 * 1024),
        name="gradient",
    )(returns, table_t, split)
    return returns.reshape(32), grad_rec


def solution(mesh):
    placed = (
        P(),
        P(None, "tp"),
        P(None, "tp"),
        P("tp"),
        P("tp"),
        P("tp"),
        P(None, "tp"),
        P("pop", None),
        P("pop"),
    )
    return jax.shard_map(
        shards, mesh=mesh, in_specs=placed, out_specs=(P("pop"), P(None, "tp")), check_vma=False
    )
```
